32 devices in a mesh: lat: 8 (over z, core), lon: 4 (over y, x).
Axes of the slice: x: 2, y: 2, z: 4, core: 2. Of those that a mesh axis runs over, the one named last changes fastest.
Arguments:
- predicted_state: float32 [1440, 13312], P('lon', 'lat'), may hold values from -24 to 24
- verified_state: float32 [1440, 13312], P('lon', 'lat'), may hold values from -20 to 20
- normal_state: float32 [1440, 13312], P('lon', 'lat'), may hold values from -3 to 3
Outputs:
- energy_curves: float32 [3, 52, 721], replicated
- rms_error: float32 [52], replicated
- anomaly_corr: float32 [52], replicated
The draws below stay inside these ranges and needn't reach their ends.
All inputs are finite; a program needn't handle non-finite values.
Results may differ from the reference program's by a relative error of at most 0.00005.
Values sent between devices are 32-bit elements; how exact they have to be, the bound alone decides.
A program may use at most 64 MiB of HBM per device.

```python
import jax
import jax.numpy as jnp
from jax import lax

VARS = 4
LEVELS = 13
NLON = 1440
FIELDS = 52
NLAT = 256


def noise_field(key):
    array_extent = (VARS * LEVELS, NLAT, NLON)
    lat_scale = 3.0 ** (jnp.arange(NLAT).astype(jnp.float32) / max(NLAT - 1, 1))
    base = jax.random.truncated_normal(key, -4.0, 4.0, array_extent, jnp.float32)
    full = base * lat_scale[None, :, None]
    return full.transpose(2, 1, 0).reshape(NLON, NLAT * VARS * LEVELS)


def draw_verified_state(key, part):
    return noise_field(jax.random.fold_in(key, 101))


def draw_predicted_state(key, part):
    shared = noise_field(jax.random.fold_in(key, 101))
    extra = noise_field(jax.random.fold_in(key, 202))
    return 0.8 * shared + 0.6 * extra


def steps_of(rng, dims, cuts, least, top_value):
    def one(axis_at, parts):
        draws = jax.random.uniform(jax.random.fold_in(jax.random.fold_in(rng, 6), axis_at), (parts,), jnp.float32, least / len(cuts), top_value / len(cuts))
        return jnp.repeat(jnp.exp(draws), dims[axis_at] // parts).reshape((-1,) + (1,) * (len(dims) - axis_at - 1))

    loudness = one(*cuts[0])
    for cut in cuts[1:]:
        loudness = loudness * one(*cut)
    return loudness


def noise(stream_key, dims, scale, limit, split=(), held_as=jnp.bfloat16):
    values = jax.random.normal(stream_key, dims, jnp.float32) * scale
    if len(split) > 0:
        values = steps_of(stream_key, dims, split, -0.22, 0.18) * values
    return jnp.clip(values, min=-limit, max=limit).astype(held_as)


def setup_inputs(seed: int = 0) -> dict:
    splits = jax.random.split(jax.random.key(seed), 4)
    return {
        "predicted_state": draw_predicted_state(jax.random.fold_in(splits[3], 71), 0),
        "verified_state": draw_verified_state(jax.random.fold_in(splits[3], 71), 0),
        "normal_state": noise(splits[2], (NLON, NLAT * FIELDS), 0.5, 3.0, ((0, 4), (1, 8)), jnp.float32),
    }


def latitude_weights(parallel_number):
    index = jnp.arange(parallel_number).astype(jnp.float32)
    return jnp.cos(jnp.pi * ((index + 0.5) / parallel_number - 0.5))

def separate_quantities(packed):
    return packed.reshape(NLON, NLAT, FIELDS).transpose(2, 1, 0)

def reference(predicted_state, verified_state, normal_state):
    predicted_state = separate_quantities(predicted_state)
    verified_state = separate_quantities(verified_state)
    normal_state = separate_quantities(normal_state)
    parallel_number = predicted_state.shape[1]
    weights = latitude_weights(parallel_number)
    weight_total = jnp.sum(weights)
    mismatch_parts = predicted_state - verified_state

    def energy_by_wavenumber(field):
        coeffs = jnp.fft.rfft(field, axis=2)
        powers = coeffs.real * coeffs.real + coeffs.imag * coeffs.imag
        return lax.optimization_barrier(jnp.sum(weights[None, :, None] * powers, axis=1)) / (NLON * NLON * weight_total)
    energy_curves = jnp.stack([energy_by_wavenumber(predicted_state), energy_by_wavenumber(verified_state), energy_by_wavenumber(mismatch_parts)])
    predicted_anomalies = predicted_state - normal_state
    observed_anomalies = verified_state - normal_state
    broad_layout = weights[None, :, None]
    normalizer = NLON * weight_total
    m_ee = lax.optimization_barrier(jnp.sum(broad_layout * mismatch_parts * mismatch_parts, axis=(1, 2))) / normalizer
    cross_moment = lax.optimization_barrier(jnp.sum(broad_layout * predicted_anomalies * observed_anomalies, axis=(1, 2))) / normalizer
    predicted_moment = lax.optimization_barrier(jnp.sum(broad_layout * predicted_anomalies * predicted_anomalies, axis=(1, 2))) / normalizer
    m_tt = lax.optimization_barrier(jnp.sum(broad_layout * observed_anomalies * observed_anomalies, axis=(1, 2))) / normalizer
    rms_error = jnp.sqrt(m_ee)
    anomaly_corr = cross_moment / jnp.sqrt((predicted_moment + 1e-06) * (m_tt + 1e-06))
    return (energy_curves, rms_error, anomaly_corr)
```

```python
import functools

import jax
import jax.numpy as jnp
import numpy as np
from jax import lax
from jax.experimental import pallas as pl
from jax.experimental.pallas import tpu as pltpu
from jax.sharding import PartitionSpec as P

FIELDS = 52
LANES = 128
MESH = pl.DeviceIdType.MESH


epsilon = 1e-06


def latitude_weights(lat_index, parallel_number):
    return jnp.cos(jnp.pi * ((lat_index.astype(jnp.float32) + 0.5) / parallel_number - 0.5))


def dft_table(lon_rows, lon_total, wave_count):
    longitudes = jnp.arange(lon_rows, dtype=jnp.int32)
    waves = jnp.arange(wave_count, dtype=jnp.int32)
    phase = longitudes[:, None] * waves[None, :] % lon_total
    angle = 2.0 * jnp.pi / lon_total * phase.astype(jnp.float32)
    return jnp.concatenate([jnp.cos(angle), -jnp.sin(angle)], axis=1)


def transform_columns(stacked, table):
    return lax.dot_general(
        stacked,
        table,
        (((0,), (0,)), ((), ())),
        precision=lax.Precision.HIGHEST,
        preferred_element_type=jnp.float32,
    )


def row_powers(fore_coeffs, true_coeffs, wave_count):
    diff_coeffs = fore_coeffs - true_coeffs

    def square(coeffs):
        return (
            coeffs[:, :wave_count] * coeffs[:, :wave_count]
            + coeffs[:, wave_count:] * coeffs[:, wave_count:]
        )

    return jnp.stack([square(fore_coeffs), square(true_coeffs), square(diff_coeffs)], axis=1)


def local(predicted_state, verified_state, normal_state):
    quantity_labels = FIELDS
    meridian_lines, meridian_number = predicted_state.shape
    parallel_lines = meridian_number // quantity_labels
    parallel_number = parallel_lines * lax.axis_size("lat")
    lon_devices = lax.axis_size("lon")
    lon_total = meridian_lines * lon_devices
    wave_count = lon_total // 2 + 1
    row_share = meridian_number // lon_devices
    lat_first = lax.axis_index("lat") * parallel_lines
    weights = latitude_weights(
        lat_first + jnp.arange(parallel_lines, dtype=jnp.int32), parallel_number
    )
    weight_total = jnp.sum(
        latitude_weights(jnp.arange(parallel_number, dtype=jnp.int32), parallel_number)
    )
    predicted_block = predicted_state.reshape(meridian_lines, parallel_lines, quantity_labels)
    observed_block = verified_state.reshape(meridian_lines, parallel_lines, quantity_labels)
    normal_block = normal_state.reshape(meridian_lines, parallel_lines, quantity_labels)
    mismatch_parts = predicted_block - observed_block
    predicted_anomalies = predicted_block - normal_block
    observed_anomalies = observed_block - normal_block
    broad_layout = weights[None, :, None]
    skill_terms = jnp.stack(
        [
            jnp.sum(broad_layout * mismatch_parts * mismatch_parts, axis=(0, 1)),
            jnp.sum(broad_layout * predicted_anomalies * observed_anomalies, axis=(0, 1)),
            jnp.sum(broad_layout * predicted_anomalies * predicted_anomalies, axis=(0, 1)),
            jnp.sum(broad_layout * observed_anomalies * observed_anomalies, axis=(0, 1)),
        ]
    )
    predicted_meridians = predicted_block.transpose(0, 2, 1).reshape(
        meridian_lines, meridian_number
    )
    true_cols = observed_block.transpose(0, 2, 1).reshape(meridian_lines, meridian_number)
    full_table = dft_table(lon_total, lon_total, wave_count)
    fore_blocks = predicted_meridians.reshape(meridian_lines, lon_devices, row_share)
    true_blocks = true_cols.reshape(meridian_lines, lon_devices, row_share)
    fore_part = lax.all_to_all(fore_blocks, "lon", split_axis=1, concat_axis=0, tiled=True)[:, 0, :]
    true_part = lax.all_to_all(true_blocks, "lon", split_axis=1, concat_axis=0, tiled=True)[:, 0, :]
    items = fore_part.shape[1]
    stacked = jnp.concatenate([fore_part, true_part], axis=1)
    coeffs = transform_columns(stacked, full_table)
    powers = row_powers(coeffs[:items], coeffs[items:], wave_count)
    share_start = lax.axis_index("lon") * row_share
    global_cols = share_start + jnp.arange(row_share, dtype=jnp.int32)
    field_of = global_cols // parallel_lines
    row_weights = latitude_weights(lat_first + global_cols % parallel_lines, parallel_number)
    row_scale = row_weights / (lon_total * lon_total * weight_total)
    weighted = powers.reshape(row_share, 3 * wave_count) * row_scale[:, None]
    field_index = jnp.arange(quantity_labels, dtype=jnp.int32)
    window = min(quantity_labels, row_share // parallel_lines + 2)
    first_field = share_start // parallel_lines
    window_index = jnp.arange(window, dtype=jnp.int32)
    offset = field_of - first_field
    selector = (offset[None, :] == window_index[:, None]).astype(jnp.float32)
    band_sum = jnp.dot(
        selector, weighted, precision=lax.Precision.HIGHEST, preferred_element_type=jnp.float32
    )
    band_sum = lax.psum(band_sum, "lat")
    gathered = lax.all_gather(band_sum, "lon", axis=0, tiled=True)
    slot_index = jnp.arange(lon_devices * window, dtype=jnp.int32)
    slot_field = slot_index // window * row_share // parallel_lines + slot_index % window
    placer = (slot_field[None, :] == field_index[:, None]).astype(jnp.float32)
    summed = jnp.dot(
        placer, gathered, precision=lax.Precision.HIGHEST, preferred_element_type=jnp.float32
    )
    energy_curves = summed.reshape(quantity_labels, 3, wave_count).transpose(1, 0, 2)
    skill_means = lax.psum(skill_terms, ("lat", "lon")) / (lon_total * weight_total)
    rms_error = jnp.sqrt(skill_means[0])
    anomaly_corr = skill_means[1] / jnp.sqrt(
        (skill_means[2] + epsilon) * (skill_means[3] + epsilon)
    )
    return (energy_curves, rms_error, anomaly_corr)


def split_np(values):
    hi = values.astype(jnp.bfloat16)
    lo = (values - hi.astype(np.float64)).astype(jnp.bfloat16)
    return hi, lo


def plan_constants(rows, cols, lat_devices, lon_devices):
    total = rows * lon_devices
    waves = total // 2 + 1
    depth = -(-rows // LANES) * LANES
    per_class = -(-(-(-waves // 4)) // 8) * 8
    table = np.zeros((4, 2 * per_class, depth), np.float64)
    lons = np.arange(rows)
    for r in range(4):
        k = np.arange(r, waves, 4)
        angle = 2.0 * np.pi * ((k[:, None] * lons[None, :]) % total) / total
        table[r, : len(k), :rows] = np.cos(angle)
        table[r, per_class : per_class + len(k), :rows] = np.sin(angle)
    hi, lo = split_np(table)
    lat_lines = cols // FIELDS
    lat_total = lat_lines * lat_devices
    all_weights = np.cos(np.pi * ((np.arange(lat_total) + 0.5) / lat_total - 0.5))
    scale = 1.0 / (float(total) * float(total) * all_weights.sum())
    tiles = cols // LANES
    piece = LANES // lon_devices
    slots = tiles + lon_devices
    col_of = np.full((slots, LANES), -1, np.int64)
    for t in range(tiles):
        col_of[t] = np.arange(LANES) + LANES * t
    for d in range(lon_devices):
        col_of[tiles + d, :piece] = (tiles - 1) * LANES + piece * d + np.arange(piece)
    valid = col_of >= 0
    field = np.where(valid, col_of % FIELDS, -1).astype(np.int32)
    weight = np.zeros((lat_devices, slots, LANES), np.float64)
    for a in range(lat_devices):
        weight[a] = np.where(valid, all_weights[a * lat_lines + np.maximum(col_of, 0) // FIELDS] * scale, 0.0)
    return hi, lo, field, weight.reshape(lat_devices * slots, LANES).astype(np.float32)


def kernel(
    dims, fore, true, norm, tab_hi, tab_lo, field, weight,
    energy, skill,
    fb, tb, nb, rx, ps, pr, bhi, blo, pbuf, acc, r0, half, r1, quart, r2, full,
    load_sem, own_sem, xs, xr, qs, qr, ss, sr,
):
    rows, cols, n_lat, n_lon, total = dims
    n_z = n_lat // 2
    lat = lax.axis_index("lat")
    lon = lax.axis_index("lon")
    core = lat % 2
    z = lat // 2
    tiles = cols // LANES
    own_tiles = tiles // n_lon
    slots = tiles + n_lon
    piece = LANES // n_lon
    depth = tab_hi.shape[2]
    per_class = tab_hi.shape[1] // 2
    waves = total // 2 + 1
    n_rows = 3 * FIELDS + 4
    sibling = {"lat": lat + 1 - 2 * core, "lon": lon}

    def lon_peer(p):
        return {"lat": lat, "lon": (lon + p) % n_lon}

    def z_peer(p):
        return {"lat": (z + p) % n_z * 2 + core, "lon": lon}

    barrier = pltpu.get_barrier_semaphore()
    peers = [sibling] + [lon_peer(p) for p in range(1, n_lon)] + [z_peer(p) for p in range(1, n_z)]
    for d in peers:
        pl.semaphore_signal(barrier, inc=1, device_id=d, device_id_type=MESH)
    loads = [
        pltpu.make_async_copy(src, dst, load_sem.at[i])
        for i, (src, dst) in enumerate(((fore, fb), (true, tb), (norm, nb)))
    ]
    for c in loads:
        c.start()
    sources = (fore, true)

    def tile_ref(a, t):
        return sources[a].at[:, pl.ds(pl.multiple_of(t * LANES, LANES), LANES)]

    own = {}
    for c in range(own_tiles):
        for a in range(2):
            own[a, c] = pltpu.make_async_copy(
                tile_ref(a, lon * own_tiles + c), rx.at[a, c, lon], own_sem.at[a, c]
            )
            own[a, c].start()
    pl.semaphore_wait(barrier, len(peers))

    sends = {}

    def send_tile(c):
        for p in (2, 1, 3) if n_lon == 4 else range(1, n_lon):
            for a in range(2):
                dest = (lon + p) % n_lon
                sends[a, c, p] = pltpu.make_async_remote_copy(
                    src_ref=tile_ref(a, dest * own_tiles + c),
                    dst_ref=rx.at[a, c, lon],
                    send_sem=xs.at[a, c, p - 1],
                    recv_sem=xr.at[a, c, p - 1],
                    device_id=lon_peer(p),
                    device_id_type=MESH,
                )
                sends[a, c, p].start()

    send_tile(0)
    loads[0].wait()
    loads[1].wait()
    last = (tiles - 1) * LANES
    pad = jnp.zeros((depth - rows, LANES), jnp.float32)
    for a, block in enumerate((fb, tb)):
        flipped = jnp.concatenate([block[:, last : last + LANES], pad], axis=0).T
        ps[a] = flipped.reshape(n_lon, piece, depth)
    for c in range(1, own_tiles):
        send_tile(c) if c == 1 else None
    for p in range(1, n_lon):
        for a in range(2):
            sends[a, "piece", p] = pltpu.make_async_remote_copy(
                src_ref=ps.at[a, (lon + p) % n_lon],
                dst_ref=pr.at[a, lon],
                send_sem=qs.at[a, p - 1],
                recv_sem=qr.at[a, p - 1],
                device_id=lon_peer(p),
                device_id_type=MESH,
            )
            sends[a, "piece", p].start()
    for c in range(2, own_tiles):
        send_tile(c)

    acc[...] = jnp.zeros_like(acc)
    pbuf[...] = jnp.zeros_like(pbuf)
    loads[2].wait()
    field_rows = lax.broadcasted_iota(jnp.int32, (LANES, LANES), 0)

    def skill_tile(t, carry):
        lanes = pl.ds(pl.multiple_of(t * LANES, LANES), LANES)
        f, v, n = fb[:, lanes], tb[:, lanes], nb[:, lanes]
        e, af, at = f - v, f - n, v - n

        def total_of(u):
            return jnp.sum(u, axis=0, keepdims=True)

        sums = jnp.concatenate(
            [jnp.zeros((4, LANES), jnp.float32), total_of(e * e), total_of(af * at), total_of(af * af), total_of(at * at)],
            axis=0,
        )
        sums = sums * (weight[pl.ds(lat * slots + t, 1), :] * float(total))
        pick = (field_rows == field[pl.ds(t, 1), :]).astype(jnp.float32)
        return carry + lax.dot_general(
            sums, pick, (((1,), (1,)), ((), ())),
            precision=lax.Precision.HIGHEST, preferred_element_type=jnp.float32,
        )

    skill_sums = lax.fori_loop(0, tiles, skill_tile, jnp.zeros((8, LANES), jnp.float32))
    acc[n_rows - 8 : n_rows, :] = skill_sums

    out_rows = lax.broadcasted_iota(jnp.int32, (n_rows, LANES), 0)

    def put(group, a, y):
        y = jnp.concatenate([y, pad], axis=0)
        hi = y.astype(jnp.bfloat16)
        lo = (y - hi.astype(jnp.float32)).astype(jnp.bfloat16)
        at = group * 2 * LANES + a * LANES
        bhi[:, at : at + LANES] = hi
        blo[:, at : at + LANES] = lo

    def product(r, start, width):
        cut = slice(start, start + width)
        th, tl = tab_hi[r], tab_lo[r]
        return (
            jnp.dot(th, bhi[:, cut], preferred_element_type=jnp.float32)
            + jnp.dot(th, blo[:, cut], preferred_element_type=jnp.float32)
            + jnp.dot(tl, bhi[:, cut], preferred_element_type=jnp.float32)
        )

    def process(c, slot):
        for a in range(2):
            x = [rx[a, c, q] for q in range(4)]
            s02, s13 = x[0] + x[2], x[1] + x[3]
            put(0, a, s02 + s13)
            put(1, a, s02 - s13)
            put(2, a, x[0] - x[2])
            put(3, a, x[1] - x[3])
        w = weight[pl.ds(lat * slots + slot, 1), :]
        for r in range(4):
            if r % 2 == 0:
                both = product(r, (r // 2) * 2 * LANES, 2 * LANES)
                re, im = both[:per_class], both[per_class:]
            else:
                both = product(r, 4 * LANES, 4 * LANES)
                u, v = both[:per_class], both[per_class:]
                g = 1.0 if r == 1 else -1.0
                re = u[:, : 2 * LANES] - g * v[:, 2 * LANES :]
                im = v[:, : 2 * LANES] + g * u[:, 2 * LANES :]
            for curve in range(3):
                if curve == 2:
                    a, b = re[:, :LANES] - re[:, LANES:], im[:, :LANES] - im[:, LANES:]
                else:
                    cut = slice(curve * LANES, (curve + 1) * LANES)
                    a, b = re[:, cut], im[:, cut]
                pbuf.at[curve][pl.ds(r, per_class, stride=4), :] = (a * a + b * b) * w
        fld = field[pl.ds(slot, 1), :]
        for curve in range(3):
            power = pbuf[curve]
            hi = power.astype(jnp.bfloat16)
            lo = (power - hi.astype(jnp.float32)).astype(jnp.bfloat16)
            pick = (out_rows == jnp.where(fld >= 0, fld + FIELDS * curve, -1)).astype(jnp.float32).astype(jnp.bfloat16)
            part = lax.dot_general(
                jnp.concatenate([pick, pick], axis=1), jnp.concatenate([hi, lo], axis=1),
                (((1,), (1,)), ((), ())), preferred_element_type=jnp.float32,
            )
            for t in range(part.shape[1] // LANES):
                acc[t * n_rows : (t + 1) * n_rows, :] += part[:, t * LANES : (t + 1) * LANES]

    def take_tile(c):
        for a in range(2):
            own[a, c].wait()
            for p in range(1, n_lon):
                sends[a, c, p].wait_recv()
        process(c, lon * own_tiles + c)

    def take_piece():
        for a in range(2):
            for p in range(1, n_lon):
                sends[a, "piece", p].wait_recv()
        gap = jnp.zeros((LANES - piece, depth), jnp.float32)
        for a in range(2):
            pr[a, lon] = ps[a, lon]
            for q in range(n_lon):
                rx[a, own_tiles, q] = jnp.concatenate([pr[a, q], gap], axis=0).T[:rows]
        process(own_tiles, tiles + lon)

    take_tile(0)
    for c in range(1, own_tiles):
        take_tile(c) if c == 1 else None
    take_piece()
    for c in range(2, own_tiles):
        take_tile(c)

    size = acc.shape[0]
    s_half, s_quart = size // 2, size // (2 * n_lon)
    s_piece = s_quart // n_z

    def exchange(index, src, dst, device):
        copy = pltpu.make_async_remote_copy(
            src_ref=src, dst_ref=dst, send_sem=ss.at[index], recv_sem=sr.at[index],
            device_id=device, device_id_type=MESH,
        )
        copy.start()
        return copy

    def part(start, length):
        return pl.ds(pl.multiple_of(start, 8), length)

    def settle(copies):
        for c in copies:
            c.wait()

    settle([exchange(0, acc.at[part((1 - core) * s_half, s_half)], r0, sibling)])
    half[...] = acc[part(core * s_half, s_half), :] + r0[...]
    settle([
        exchange(p, half.at[part((lon + p) % n_lon * s_quart, s_quart)], r1.at[p - 1], lon_peer(p))
        for p in range(1, n_lon)
    ])
    quart[...] = half[part(lon * s_quart, s_quart), :] + r1[0] + r1[1] + r1[2]
    base = n_lon
    settle([
        exchange(base + p - 1, quart.at[part((z + p) % n_z * s_piece, s_piece)], r2.at[p - 1], z_peer(p))
        for p in range(1, n_z)
    ])
    done = quart[part(z * s_piece, s_piece), :]
    for p in range(1, n_z):
        done = done + r2[p - 1]
    mine = part(core * s_half + lon * s_quart + z * s_piece, s_piece)
    full[mine, :] = done
    base += n_z - 1
    settle([exchange(base + p - 1, full.at[mine], full.at[mine], z_peer(p)) for p in range(1, n_z)])
    base += n_z - 1
    mine = part(core * s_half + lon * s_quart, s_quart)
    settle([exchange(base + p - 1, full.at[mine], full.at[mine], lon_peer(p)) for p in range(1, n_lon)])
    base += n_lon - 1
    mine = part(core * s_half, s_half)
    settle([exchange(base, full.at[mine], full.at[mine], sibling)])
    for c in sends.values():
        c.wait_send()

    for t in range(-(-waves // LANES)):
        width = min(LANES, waves - t * LANES)
        for curve in range(3):
            at = t * n_rows + curve * FIELDS
            energy[curve, :, t * LANES : t * LANES + width] = full[at : at + FIELDS, :width]
    means = full[n_rows - 4 : n_rows, :]
    m_ee, m_ft, m_ff, m_tt = means[0:1], means[1:2], means[2:3], means[3:4]
    skill[0:1, :] = jnp.sqrt(m_ee)
    skill[1:2, :] = m_ft / jnp.sqrt((m_ff + epsilon) * (m_tt + epsilon))


def fused(lat_devices, lon_devices, predicted_state, verified_state, normal_state):
    rows, cols = predicted_state.shape
    total = rows * lon_devices
    waves = total // 2 + 1
    tab_hi, tab_lo, field, weight = plan_constants(rows, cols, lat_devices, lon_devices)
    depth = tab_hi.shape[2]
    per_class = tab_hi.shape[1] // 2
    tiles = cols // LANES
    own_tiles = tiles // lon_devices
    piece = LANES // lon_devices
    spread = -(-4 * per_class // LANES) * LANES
    n_rows = 3 * FIELDS + 4
    n_z = lat_devices // 2
    unit = 8 * lat_devices * lon_devices
    size = -(-(spread // LANES) * n_rows // unit) * unit
    f32, b16 = jnp.float32, jnp.bfloat16
    copies = 2 * (lon_devices + n_z - 1)
    dma = pltpu.SemaphoreType.DMA
    scratch = [
        pltpu.VMEM((rows, cols), f32), pltpu.VMEM((rows, cols), f32), pltpu.VMEM((rows, cols), f32),
        pltpu.VMEM((2, own_tiles + 1, lon_devices, rows, LANES), f32),
        pltpu.VMEM((2, lon_devices, piece, depth), f32),
        pltpu.VMEM((2, lon_devices, piece, depth), f32),
        pltpu.VMEM((depth, 8 * LANES), b16), pltpu.VMEM((depth, 8 * LANES), b16),
        pltpu.VMEM((3, spread, LANES), f32),
        pltpu.VMEM((size, LANES), f32),
        pltpu.VMEM((size // 2, LANES), f32), pltpu.VMEM((size // 2, LANES), f32),
        pltpu.VMEM((lon_devices - 1, size // (2 * lon_devices), LANES), f32),
        pltpu.VMEM((size // (2 * lon_devices), LANES), f32),
        pltpu.VMEM((n_z - 1, size // (2 * lon_devices * n_z), LANES), f32),
        pltpu.VMEM((size, LANES), f32),
        dma((3,)), dma((2, own_tiles)),
        dma((2, own_tiles, lon_devices - 1)), dma((2, own_tiles, lon_devices - 1)),
        dma((2, lon_devices - 1)), dma((2, lon_devices - 1)),
        dma((copies,)), dma((copies,)),
    ]
    any_spec = pl.BlockSpec(memory_space=pl.ANY)
    vmem = pl.BlockSpec(memory_space=pltpu.VMEM)
    dims = (rows, cols, lat_devices, lon_devices, total)
    energy, skill = pl.pallas_call(
        functools.partial(kernel, dims),
        out_shape=(
            jax.ShapeDtypeStruct((3, FIELDS, waves), f32),
            jax.ShapeDtypeStruct((2, LANES), f32),
        ),
        in_specs=[any_spec] * 3 + [vmem] * 4,
        out_specs=(vmem, vmem),
        scratch_shapes=scratch,
        compiler_params=pltpu.CompilerParams(
            collective_id=0, has_side_effects=True, vmem_limit_bytes=60_000_000
        ),
    )(predicted_state, verified_state, normal_state, jnp.asarray(tab_hi), jnp.asarray(tab_lo), jnp.asarray(field), jnp.asarray(weight))
    return energy, skill[0, :FIELDS], skill[1, :FIELDS]


def solution(mesh):
    in_specs = (P("lon", "lat"), P("lon", "lat"), P("lon", "lat"))
    out_specs = (P(), P(), P())
    n_lat, n_lon = mesh.shape["lat"], mesh.shape["lon"]

    def body(predicted_state, verified_state, normal_state):
        rows, cols = predicted_state.shape
        fits = (
            n_lon == 4 and n_lat % 2 == 0 and n_lat > 2 and rows % 8 == 0
            and cols % LANES == 0 and cols // LANES % n_lon == 1 and cols // LANES // n_lon >= 2
        )
        if fits:
            return fused(n_lat, n_lon, predicted_state, verified_state, normal_state)
        return local(predicted_state, verified_state, normal_state)

    return jax.shard_map(body, mesh=mesh, in_specs=in_specs, out_specs=out_specs, check_vma=False)
```

```python
import functools

import jax
import jax.numpy as jnp
import numpy as np
from jax import lax
from jax.experimental import pallas as pl
from jax.experimental.pallas import tpu as pltpu
from jax.sharding import PartitionSpec as P

FIELDS = 52
LANES = 128
MESH = pl.DeviceIdType.MESH
ORDER = (3, 1, 2)


epsilon = 1e-06


def latitude_weights(lat_index, parallel_number):
    return jnp.cos(jnp.pi * ((lat_index.astype(jnp.float32) + 0.5) / parallel_number - 0.5))


def dft_table(lon_rows, lon_total, wave_count):
    longitudes = jnp.arange(lon_rows, dtype=jnp.int32)
    waves = jnp.arange(wave_count, dtype=jnp.int32)
    phase = longitudes[:, None] * waves[None, :] % lon_total
    angle = 2.0 * jnp.pi / lon_total * phase.astype(jnp.float32)
    return jnp.concatenate([jnp.cos(angle), -jnp.sin(angle)], axis=1)


def transform_columns(stacked, table):
    return lax.dot_general(
        stacked,
        table,
        (((0,), (0,)), ((), ())),
        precision=lax.Precision.HIGHEST,
        preferred_element_type=jnp.float32,
    )


def row_powers(fore_coeffs, true_coeffs, wave_count):
    diff_coeffs = fore_coeffs - true_coeffs

    def square(coeffs):
        return (
            coeffs[:, :wave_count] * coeffs[:, :wave_count]
            + coeffs[:, wave_count:] * coeffs[:, wave_count:]
        )

    return jnp.stack([square(fore_coeffs), square(true_coeffs), square(diff_coeffs)], axis=1)


def local(predicted_state, verified_state, normal_state):
    quantity_labels = FIELDS
    meridian_lines, meridian_number = predicted_state.shape
    parallel_lines = meridian_number // quantity_labels
    parallel_number = parallel_lines * lax.axis_size("lat")
    lon_devices = lax.axis_size("lon")
    lon_total = meridian_lines * lon_devices
    wave_count = lon_total // 2 + 1
    row_share = meridian_number // lon_devices
    lat_first = lax.axis_index("lat") * parallel_lines
    weights = latitude_weights(
        lat_first + jnp.arange(parallel_lines, dtype=jnp.int32), parallel_number
    )
    weight_total = jnp.sum(
        latitude_weights(jnp.arange(parallel_number, dtype=jnp.int32), parallel_number)
    )
    predicted_block = predicted_state.reshape(meridian_lines, parallel_lines, quantity_labels)
    observed_block = verified_state.reshape(meridian_lines, parallel_lines, quantity_labels)
    normal_block = normal_state.reshape(meridian_lines, parallel_lines, quantity_labels)
    mismatch_parts = predicted_block - observed_block
    predicted_anomalies = predicted_block - normal_block
    observed_anomalies = observed_block - normal_block
    broad_layout = weights[None, :, None]
    skill_terms = jnp.stack(
        [
            jnp.sum(broad_layout * mismatch_parts * mismatch_parts, axis=(0, 1)),
            jnp.sum(broad_layout * predicted_anomalies * observed_anomalies, axis=(0, 1)),
            jnp.sum(broad_layout * predicted_anomalies * predicted_anomalies, axis=(0, 1)),
            jnp.sum(broad_layout * observed_anomalies * observed_anomalies, axis=(0, 1)),
        ]
    )
    predicted_meridians = predicted_block.transpose(0, 2, 1).reshape(
        meridian_lines, meridian_number
    )
    true_cols = observed_block.transpose(0, 2, 1).reshape(meridian_lines, meridian_number)
    full_table = dft_table(lon_total, lon_total, wave_count)
    fore_blocks = predicted_meridians.reshape(meridian_lines, lon_devices, row_share)
    true_blocks = true_cols.reshape(meridian_lines, lon_devices, row_share)
    fore_part = lax.all_to_all(fore_blocks, "lon", split_axis=1, concat_axis=0, tiled=True)[:, 0, :]
    true_part = lax.all_to_all(true_blocks, "lon", split_axis=1, concat_axis=0, tiled=True)[:, 0, :]
    items = fore_part.shape[1]
    stacked = jnp.concatenate([fore_part, true_part], axis=1)
    coeffs = transform_columns(stacked, full_table)
    powers = row_powers(coeffs[:items], coeffs[items:], wave_count)
    share_start = lax.axis_index("lon") * row_share
    global_cols = share_start + jnp.arange(row_share, dtype=jnp.int32)
    field_of = global_cols // parallel_lines
    row_weights = latitude_weights(lat_first + global_cols % parallel_lines, parallel_number)
    row_scale = row_weights / (lon_total * lon_total * weight_total)
    weighted = powers.reshape(row_share, 3 * wave_count) * row_scale[:, None]
    field_index = jnp.arange(quantity_labels, dtype=jnp.int32)
    window = min(quantity_labels, row_share // parallel_lines + 2)
    first_field = share_start // parallel_lines
    window_index = jnp.arange(window, dtype=jnp.int32)
    offset = field_of - first_field
    selector = (offset[None, :] == window_index[:, None]).astype(jnp.float32)
    band_sum = jnp.dot(
        selector, weighted, precision=lax.Precision.HIGHEST, preferred_element_type=jnp.float32
    )
    band_sum = lax.psum(band_sum, "lat")
    gathered = lax.all_gather(band_sum, "lon", axis=0, tiled=True)
    slot_index = jnp.arange(lon_devices * window, dtype=jnp.int32)
    slot_field = slot_index // window * row_share // parallel_lines + slot_index % window
    placer = (slot_field[None, :] == field_index[:, None]).astype(jnp.float32)
    summed = jnp.dot(
        placer, gathered, precision=lax.Precision.HIGHEST, preferred_element_type=jnp.float32
    )
    energy_curves = summed.reshape(quantity_labels, 3, wave_count).transpose(1, 0, 2)
    skill_means = lax.psum(skill_terms, ("lat", "lon")) / (lon_total * weight_total)
    rms_error = jnp.sqrt(skill_means[0])
    anomaly_corr = skill_means[1] / jnp.sqrt(
        (skill_means[2] + epsilon) * (skill_means[3] + epsilon)
    )
    return (energy_curves, rms_error, anomaly_corr)


def split_np(values):
    hi = values.astype(jnp.bfloat16)
    lo = (values - hi.astype(np.float64)).astype(jnp.bfloat16)
    return hi, lo


def plan_constants(rows, cols, lat_devices, lon_devices):
    total = rows * lon_devices
    waves = total // 2 + 1
    depth = -(-rows // LANES) * LANES
    per_class = -(-(-(-waves // 4)) // 8) * 8
    table = np.zeros((4, 2 * per_class, depth), np.float64)
    lons = np.arange(rows)
    for r in range(4):
        k = np.arange(r, waves, 4)
        angle = 2.0 * np.pi * ((k[:, None] * lons[None, :]) % total) / total
        table[r, : len(k), :rows] = np.cos(angle)
        table[r, per_class : per_class + len(k), :rows] = np.sin(angle)
    hi, lo = split_np(table)
    lat_lines = cols // FIELDS
    lat_total = lat_lines * lat_devices
    all_weights = np.cos(np.pi * ((np.arange(lat_total) + 0.5) / lat_total - 0.5))
    scale = 1.0 / (float(total) * float(total) * all_weights.sum())
    tiles = cols // LANES
    piece = LANES // lon_devices
    slots = tiles + lon_devices
    col_of = np.full((slots, LANES), -1, np.int64)
    for t in range(tiles):
        col_of[t] = np.arange(LANES) + LANES * t
    for d in range(lon_devices):
        col_of[tiles + d, :piece] = (tiles - 1) * LANES + piece * d + np.arange(piece)
    valid = col_of >= 0
    field = np.where(valid, col_of % FIELDS, -1).astype(np.int32)
    weight = np.zeros((lat_devices, slots, LANES), np.float64)
    for a in range(lat_devices):
        weight[a] = np.where(valid, all_weights[a * lat_lines + np.maximum(col_of, 0) // FIELDS] * scale, 0.0)
    return hi, lo, field, weight.reshape(lat_devices * slots, LANES).astype(np.float32)


def kernel(
    dims, fore, true, norm, hi_hbm, lo_hbm, field, weight,
    result,
    fb, tb, nb, rx, ps, pr, bhi, blo, pbuf, acc, r0, half, r1, quart, r2, full,
    load_sem, own_sem, xs, xr, qs, qr, ss, sr, tab_hi, tab_lo,
):
    rows, cols, n_lat, n_lon, total = dims
    n_z = n_lat // 2
    lat = lax.axis_index("lat")
    lon = lax.axis_index("lon")
    core = lat % 2
    z = lat // 2
    tiles = cols // LANES
    own_tiles = tiles // n_lon
    slots = tiles + n_lon
    piece = LANES // n_lon
    depth = tab_hi.shape[2]
    per_class = tab_hi.shape[1] // 2
    waves = total // 2 + 1
    n_rows = 3 * FIELDS + 4
    sibling = {"lat": lat + 1 - 2 * core, "lon": lon}

    flips = (lon, lon + 1 - 2 * (lon % 2), lon + 2 - 4 * (lon // 2), n_lon - 1 - lon)

    def lon_peer(p):
        return {"lat": lat, "lon": flips[p]}

    def z_peer(p):
        return {"lat": (z + p) % n_z * 2 + core, "lon": lon}

    barrier = pltpu.get_barrier_semaphore()
    peers = [sibling] + [lon_peer(p) for p in range(1, n_lon)] + [z_peer(p) for p in range(1, n_z)]
    for d in peers:
        pl.semaphore_signal(barrier, inc=1, device_id=d, device_id_type=MESH)
    loads = [
        pltpu.make_async_copy(src, dst, load_sem.at[i])
        for i, (src, dst) in enumerate(((fore, fb), (true, tb), (norm, nb), (hi_hbm, tab_hi), (lo_hbm, tab_lo)))
    ]
    for c in loads:
        c.start()
    sources = (fore, true)

    def tile_ref(a, t):
        return sources[a].at[:, pl.ds(pl.multiple_of(t * LANES, LANES), LANES)]

    own = {}
    for c in range(own_tiles):
        for a in range(2):
            own[a, c] = pltpu.make_async_copy(
                tile_ref(a, lon * own_tiles + c), rx.at[a, c, lon], own_sem.at[a, c]
            )
            own[a, c].start()
    pl.semaphore_wait(barrier, len(peers))

    sends = {}

    def send_tile(c):
        for p in ORDER:
            for a in range(2):
                dest = flips[p]
                sends[a, c, p] = pltpu.make_async_remote_copy(
                    src_ref=tile_ref(a, dest * own_tiles + c),
                    dst_ref=rx.at[a, c, lon],
                    send_sem=xs.at[a, c, p - 1],
                    recv_sem=xr.at[a, c, p - 1],
                    device_id=lon_peer(p),
                    device_id_type=MESH,
                )
                sends[a, c, p].start()

    send_tile(0)
    loads[0].wait()
    loads[1].wait()
    last = (tiles - 1) * LANES
    pad = jnp.zeros((depth - rows, LANES), jnp.float32)
    for a, block in enumerate((fb, tb)):
        flipped = jnp.concatenate([block[:, last : last + LANES], pad], axis=0).T
        ps[a] = flipped.reshape(n_lon, piece, depth)
    for c in range(1, own_tiles):
        send_tile(c) if c == 1 else None
    for p in ORDER:
        for a in range(2):
            sends[a, "piece", p] = pltpu.make_async_remote_copy(
                src_ref=ps.at[a, flips[p]],
                dst_ref=pr.at[a, lon],
                send_sem=qs.at[a, p - 1],
                recv_sem=qr.at[a, p - 1],
                device_id=lon_peer(p),
                device_id_type=MESH,
            )
            sends[a, "piece", p].start()
    for c in range(2, own_tiles):
        send_tile(c)

    acc[...] = jnp.zeros_like(acc)
    pbuf[...] = jnp.zeros_like(pbuf)
    loads[2].wait()
    field_rows = lax.broadcasted_iota(jnp.int32, (LANES, LANES), 0)

    def skill_tile(t, carry):
        lanes = pl.ds(pl.multiple_of(t * LANES, LANES), LANES)
        f, v, n = fb[:, lanes], tb[:, lanes], nb[:, lanes]
        e, af, at = f - v, f - n, v - n

        def total_of(u):
            return jnp.sum(u, axis=0, keepdims=True)

        sums = jnp.concatenate(
            [jnp.zeros((4, LANES), jnp.float32), total_of(e * e), total_of(af * at), total_of(af * af), total_of(at * at)],
            axis=0,
        )
        sums = sums * (weight[pl.ds(lat * slots + t, 1), :] * float(total))
        pick = (field_rows == field[pl.ds(t, 1), :]).astype(jnp.float32)
        return carry + lax.dot_general(
            sums, pick, (((1,), (1,)), ((), ())),
            precision=lax.Precision.HIGHEST, preferred_element_type=jnp.float32,
        )

    skill_sums = lax.fori_loop(0, tiles, skill_tile, jnp.zeros((8, LANES), jnp.float32))
    acc[n_rows - 8 : n_rows, :] = skill_sums

    out_rows = lax.broadcasted_iota(jnp.int32, (n_rows, LANES), 0)

    def put(group, a, y):
        y = jnp.concatenate([y, pad], axis=0)
        hi = y.astype(jnp.bfloat16)
        lo = (y - hi.astype(jnp.float32)).astype(jnp.bfloat16)
        at = group * 2 * LANES + a * LANES
        bhi[:, at : at + LANES] = hi
        blo[:, at : at + LANES] = lo

    def product(r, start, width):
        cut = slice(start, start + width)
        th, tl = tab_hi[r], tab_lo[r]
        return (
            jnp.dot(th, bhi[:, cut], preferred_element_type=jnp.float32)
            + jnp.dot(th, blo[:, cut], preferred_element_type=jnp.float32)
            + jnp.dot(tl, bhi[:, cut], preferred_element_type=jnp.float32)
        )

    def process(c, slot):
        for a in range(2):
            x = [rx[a, c, q] for q in range(4)]
            s02, s13 = x[0] + x[2], x[1] + x[3]
            put(0, a, s02 + s13)
            put(1, a, s02 - s13)
            put(2, a, x[0] - x[2])
            put(3, a, x[1] - x[3])
        w = weight[pl.ds(lat * slots + slot, 1), :]
        for r in range(4):
            if r % 2 == 0:
                both = product(r, (r // 2) * 2 * LANES, 2 * LANES)
                re, im = both[:per_class], both[per_class:]
            else:
                both = product(r, 4 * LANES, 4 * LANES)
                u, v = both[:per_class], both[per_class:]
                g = 1.0 if r == 1 else -1.0
                re = u[:, : 2 * LANES] - g * v[:, 2 * LANES :]
                im = v[:, : 2 * LANES] + g * u[:, 2 * LANES :]
            for curve in range(3):
                if curve == 2:
                    a, b = re[:, :LANES] - re[:, LANES:], im[:, :LANES] - im[:, LANES:]
                else:
                    cut = slice(curve * LANES, (curve + 1) * LANES)
                    a, b = re[:, cut], im[:, cut]
                pbuf.at[curve][pl.ds(r, per_class, stride=4), :] = (a * a + b * b) * w
        fld = field[pl.ds(slot, 1), :]
        for curve in range(3):
            power = pbuf[curve]
            hi = power.astype(jnp.bfloat16)
            lo = (power - hi.astype(jnp.float32)).astype(jnp.bfloat16)
            pick = (out_rows == jnp.where(fld >= 0, fld + FIELDS * curve, -1)).astype(jnp.float32).astype(jnp.bfloat16)
            part = lax.dot_general(
                jnp.concatenate([pick, pick], axis=1), jnp.concatenate([hi, lo], axis=1),
                (((1,), (1,)), ((), ())), preferred_element_type=jnp.float32,
            )
            for t in range(part.shape[1] // LANES):
                acc[t * n_rows : (t + 1) * n_rows, :] += part[:, t * LANES : (t + 1) * LANES]

    def take_tile(c):
        for a in range(2):
            own[a, c].wait()
            for p in range(1, n_lon):
                sends[a, c, p].wait_recv()
        process(c, lon * own_tiles + c)

    def take_piece():
        for a in range(2):
            for p in range(1, n_lon):
                sends[a, "piece", p].wait_recv()
        gap = jnp.zeros((LANES - piece, depth), jnp.float32)
        for a in range(2):
            pr[a, lon] = ps[a, lon]
            for q in range(n_lon):
                rx[a, own_tiles, q] = jnp.concatenate([pr[a, q], gap], axis=0).T[:rows]
        process(own_tiles, tiles + lon)

    loads[3].wait()
    loads[4].wait()
    take_tile(0)
    for c in range(1, own_tiles):
        take_tile(c) if c == 1 else None
    take_piece()
    for c in range(2, own_tiles):
        take_tile(c)

    size = acc.shape[0]
    s_half, s_quart = size // 2, size // (2 * n_lon)
    s_piece = s_quart // n_z

    def exchange(index, src, dst, device):
        copy = pltpu.make_async_remote_copy(
            src_ref=src, dst_ref=dst, send_sem=ss.at[index], recv_sem=sr.at[index],
            device_id=device, device_id_type=MESH,
        )
        copy.start()
        return copy

    def part(start, length):
        return pl.ds(pl.multiple_of(start, 8), length)

    def quarter(j):
        return flips[j] * s_quart

    near_first, far_first = (1, 2, 3), (3, 1, 2)
    z_order = (2, 1, 3, 0)
    cross = {
        j: exchange(
            j, acc.at[part((1 - core) * s_half + quarter(j), s_quart)],
            r0.at[part(quarter(j), s_quart)], sibling,
        )
        for j in (*far_first, 0)
    }
    base = n_lon
    over_lon = {}
    for j in (*far_first, 0):
        cross[j].wait_recv()
        rows_j = part(quarter(j), s_quart)
        half[rows_j, :] = acc[part(core * s_half + quarter(j), s_quart), :] + r0[rows_j, :]
        if j > 0:
            for p in z_order:
                at = (z + p) % n_z * s_piece
                over_lon[j, p] = exchange(
                    base + (j - 1) * n_z + p, half.at[part(quarter(j) + at, s_piece)],
                    r1.at[j - 1, part(at, s_piece)], lon_peer(j),
                )
    base += (n_lon - 1) * n_z
    over_z = {}
    for p in z_order:
        for j in range(1, n_lon):
            over_lon[j, p].wait_recv()
        at = (z + p) % n_z * s_piece
        rows_p = part(at, s_piece)
        quart[rows_p, :] = (
            half[part(quarter(0) + at, s_piece), :] + r1[0, rows_p, :] + r1[1, rows_p, :] + r1[2, rows_p, :]
        )
        if p > 0:
            over_z[p] = exchange(base + p - 1, quart.at[rows_p], r2.at[p - 1], z_peer(p))
    base += n_z - 1
    done = quart[part(z * s_piece, s_piece), :]
    for p in range(1, n_z):
        over_z[p].wait_recv()
        done = done + r2[p - 1]
    quarter_at = core * s_half + quarter(0)
    mine = part(quarter_at + z * s_piece, s_piece)
    full[mine, :] = done

    back_z = {p: exchange(base + p - 1, full.at[mine], full.at[mine], z_peer(p)) for p in (2, 1, 3)}
    base += n_z - 1
    back_lon = {}
    for p in (0, 1, 3, 2):
        if p > 0:
            back_z[p].wait_recv()
        rows_p = part(quarter_at + (z + n_z - p) % n_z * s_piece, s_piece)
        for j in far_first:
            back_lon[j, p] = exchange(base + (j - 1) * n_z + p, full.at[rows_p], full.at[rows_p], lon_peer(j))
    base += (n_lon - 1) * n_z
    back_core = {}
    for j in (0, *near_first):
        if j > 0:
            for p in range(n_z):
                back_lon[j, p].wait_recv()
        rows_j = part(core * s_half + quarter(j), s_quart)
        back_core[j] = exchange(base + j, full.at[rows_j], full.at[rows_j], sibling)
    for c in back_core.values():
        c.wait_recv()
    for group in (cross, over_lon, over_z, back_z, back_lon, back_core):
        for c in group.values():
            c.wait_send()
    for c in sends.values():
        c.wait_send()

    result[...] = full[...]


def finish(waves, full, energy, rms, corr):
    n_rows = 3 * FIELDS + 4
    for t in range(-(-waves // LANES)):
        width = min(LANES, waves - t * LANES)
        for curve in range(3):
            at = t * n_rows + curve * FIELDS
            energy[curve, :, t * LANES : t * LANES + width] = full[at : at + FIELDS, :width]
    means = full[n_rows - 4 : n_rows, :]
    m_ee, m_ft, m_ff, m_tt = means[0:1], means[1:2], means[2:3], means[3:4]
    rms[...] = jnp.sqrt(m_ee)[0, :FIELDS]
    corr[...] = (m_ft / jnp.sqrt((m_ff + epsilon) * (m_tt + epsilon)))[0, :FIELDS]


def fused(lat_devices, lon_devices, predicted_state, verified_state, normal_state):
    rows, cols = predicted_state.shape
    total = rows * lon_devices
    waves = total // 2 + 1
    tab_hi, tab_lo, field, weight = plan_constants(rows, cols, lat_devices, lon_devices)
    depth = tab_hi.shape[2]
    per_class = tab_hi.shape[1] // 2
    tiles = cols // LANES
    own_tiles = tiles // lon_devices
    piece = LANES // lon_devices
    spread = -(-4 * per_class // LANES) * LANES
    n_rows = 3 * FIELDS + 4
    n_z = lat_devices // 2
    unit = 8 * lat_devices * lon_devices
    size = -(-(spread // LANES) * n_rows // unit) * unit
    f32, b16 = jnp.float32, jnp.bfloat16
    copies = 2 * (lon_devices + lon_devices * n_z)
    dma = pltpu.SemaphoreType.DMA
    scratch = [
        pltpu.VMEM((rows, cols), f32), pltpu.VMEM((rows, cols), f32), pltpu.VMEM((rows, cols), f32),
        pltpu.VMEM((2, own_tiles + 1, lon_devices, rows, LANES), f32),
        pltpu.VMEM((2, lon_devices, piece, depth), f32),
        pltpu.VMEM((2, lon_devices, piece, depth), f32),
        pltpu.VMEM((depth, 8 * LANES), b16), pltpu.VMEM((depth, 8 * LANES), b16),
        pltpu.VMEM((3, spread, LANES), f32),
        pltpu.VMEM((size, LANES), f32),
        pltpu.VMEM((size // 2, LANES), f32), pltpu.VMEM((size // 2, LANES), f32),
        pltpu.VMEM((lon_devices - 1, size // (2 * lon_devices), LANES), f32),
        pltpu.VMEM((size // (2 * lon_devices), LANES), f32),
        pltpu.VMEM((n_z - 1, size // (2 * lon_devices * n_z), LANES), f32),
        pltpu.VMEM((size, LANES), f32),
        dma((5,)), dma((2, own_tiles)),
        dma((2, own_tiles, lon_devices - 1)), dma((2, own_tiles, lon_devices - 1)),
        dma((2, lon_devices - 1)), dma((2, lon_devices - 1)),
        dma((copies,)), dma((copies,)),
        pltpu.VMEM(tab_hi.shape, b16), pltpu.VMEM(tab_lo.shape, b16),
    ]
    any_spec = pl.BlockSpec(memory_space=pl.ANY)
    vmem = pl.BlockSpec(memory_space=pltpu.VMEM)
    dims = (rows, cols, lat_devices, lon_devices, total)
    summed = pl.pallas_call(
        functools.partial(kernel, dims),
        out_shape=jax.ShapeDtypeStruct((size, LANES), f32),
        in_specs=[any_spec] * 5 + [vmem] * 2,
        out_specs=vmem,
        scratch_shapes=scratch,
        compiler_params=pltpu.CompilerParams(
            collective_id=0, has_side_effects=True, vmem_limit_bytes=60_000_000
        ),
    )(predicted_state, verified_state, normal_state, jnp.asarray(tab_hi), jnp.asarray(tab_lo), jnp.asarray(field), jnp.asarray(weight))
    return pl.pallas_call(
        functools.partial(finish, waves),
        out_shape=(
            jax.ShapeDtypeStruct((3, FIELDS, waves), f32),
            jax.ShapeDtypeStruct((FIELDS,), f32),
            jax.ShapeDtypeStruct((FIELDS,), f32),
        ),
        in_specs=[vmem],
        out_specs=(vmem, vmem, vmem),
    )(summed)


def solution(mesh):
    in_specs = (P("lon", "lat"), P("lon", "lat"), P("lon", "lat"))
    out_specs = (P(), P(), P())
    n_lat, n_lon = mesh.shape["lat"], mesh.shape["lon"]

    def body(predicted_state, verified_state, normal_state):
        rows, cols = predicted_state.shape
        fits = (
            n_lon == 4 and n_lat % 2 == 0 and n_lat > 2 and rows % 8 == 0
            and cols % LANES == 0 and cols // LANES % n_lon == 1 and cols // LANES // n_lon >= 2
        )
        if fits:
            return fused(n_lat, n_lon, predicted_state, verified_state, normal_state)
        return local(predicted_state, verified_state, normal_state)

    return jax.shard_map(body, mesh=mesh, in_specs=in_specs, out_specs=out_specs, check_vma=False)
```

```python
import functools

import jax
import jax.numpy as jnp
import numpy as np
from jax import lax
from jax.experimental import pallas as pl
from jax.experimental.pallas import tpu as pltpu
from jax.sharding import PartitionSpec as P

FIELDS = 52
LANES = 128
MESH = pl.DeviceIdType.MESH
ORDER = (3, 1, 2)


epsilon = 1e-06


def latitude_weights(lat_index, parallel_number):
    return jnp.cos(jnp.pi * ((lat_index.astype(jnp.float32) + 0.5) / parallel_number - 0.5))


def dft_table(lon_rows, lon_total, wave_count):
    longitudes = jnp.arange(lon_rows, dtype=jnp.int32)
    waves = jnp.arange(wave_count, dtype=jnp.int32)
    phase = longitudes[:, None] * waves[None, :] % lon_total
    angle = 2.0 * jnp.pi / lon_total * phase.astype(jnp.float32)
    return jnp.concatenate([jnp.cos(angle), -jnp.sin(angle)], axis=1)


def transform_columns(stacked, table):
    return lax.dot_general(
        stacked,
        table,
        (((0,), (0,)), ((), ())),
        precision=lax.Precision.HIGHEST,
        preferred_element_type=jnp.float32,
    )


def row_powers(fore_coeffs, true_coeffs, wave_count):
    diff_coeffs = fore_coeffs - true_coeffs

    def square(coeffs):
        return (
            coeffs[:, :wave_count] * coeffs[:, :wave_count]
            + coeffs[:, wave_count:] * coeffs[:, wave_count:]
        )

    return jnp.stack([square(fore_coeffs), square(true_coeffs), square(diff_coeffs)], axis=1)


def local(predicted_state, verified_state, normal_state):
    quantity_labels = FIELDS
    meridian_lines, meridian_number = predicted_state.shape
    parallel_lines = meridian_number // quantity_labels
    parallel_number = parallel_lines * lax.axis_size("lat")
    lon_devices = lax.axis_size("lon")
    lon_total = meridian_lines * lon_devices
    wave_count = lon_total // 2 + 1
    row_share = meridian_number // lon_devices
    lat_first = lax.axis_index("lat") * parallel_lines
    weights = latitude_weights(
        lat_first + jnp.arange(parallel_lines, dtype=jnp.int32), parallel_number
    )
    weight_total = jnp.sum(
        latitude_weights(jnp.arange(parallel_number, dtype=jnp.int32), parallel_number)
    )
    predicted_block = predicted_state.reshape(meridian_lines, parallel_lines, quantity_labels)
    observed_block = verified_state.reshape(meridian_lines, parallel_lines, quantity_labels)
    normal_block = normal_state.reshape(meridian_lines, parallel_lines, quantity_labels)
    mismatch_parts = predicted_block - observed_block
    predicted_anomalies = predicted_block - normal_block
    observed_anomalies = observed_block - normal_block
    broad_layout = weights[None, :, None]
    skill_terms = jnp.stack(
        [
            jnp.sum(broad_layout * mismatch_parts * mismatch_parts, axis=(0, 1)),
            jnp.sum(broad_layout * predicted_anomalies * observed_anomalies, axis=(0, 1)),
            jnp.sum(broad_layout * predicted_anomalies * predicted_anomalies, axis=(0, 1)),
            jnp.sum(broad_layout * observed_anomalies * observed_anomalies, axis=(0, 1)),
        ]
    )
    predicted_meridians = predicted_block.transpose(0, 2, 1).reshape(
        meridian_lines, meridian_number
    )
    true_cols = observed_block.transpose(0, 2, 1).reshape(meridian_lines, meridian_number)
    full_table = dft_table(lon_total, lon_total, wave_count)
    fore_blocks = predicted_meridians.reshape(meridian_lines, lon_devices, row_share)
    true_blocks = true_cols.reshape(meridian_lines, lon_devices, row_share)
    fore_part = lax.all_to_all(fore_blocks, "lon", split_axis=1, concat_axis=0, tiled=True)[:, 0, :]
    true_part = lax.all_to_all(true_blocks, "lon", split_axis=1, concat_axis=0, tiled=True)[:, 0, :]
    items = fore_part.shape[1]
    stacked = jnp.concatenate([fore_part, true_part], axis=1)
    coeffs = transform_columns(stacked, full_table)
    powers = row_powers(coeffs[:items], coeffs[items:], wave_count)
    share_start = lax.axis_index("lon") * row_share
    global_cols = share_start + jnp.arange(row_share, dtype=jnp.int32)
    field_of = global_cols // parallel_lines
    row_weights = latitude_weights(lat_first + global_cols % parallel_lines, parallel_number)
    row_scale = row_weights / (lon_total * lon_total * weight_total)
    weighted = powers.reshape(row_share, 3 * wave_count) * row_scale[:, None]
    field_index = jnp.arange(quantity_labels, dtype=jnp.int32)
    window = min(quantity_labels, row_share // parallel_lines + 2)
    first_field = share_start // parallel_lines
    window_index = jnp.arange(window, dtype=jnp.int32)
    offset = field_of - first_field
    selector = (offset[None, :] == window_index[:, None]).astype(jnp.float32)
    band_sum = jnp.dot(
        selector, weighted, precision=lax.Precision.HIGHEST, preferred_element_type=jnp.float32
    )
    band_sum = lax.psum(band_sum, "lat")
    gathered = lax.all_gather(band_sum, "lon", axis=0, tiled=True)
    slot_index = jnp.arange(lon_devices * window, dtype=jnp.int32)
    slot_field = slot_index // window * row_share // parallel_lines + slot_index % window
    placer = (slot_field[None, :] == field_index[:, None]).astype(jnp.float32)
    summed = jnp.dot(
        placer, gathered, precision=lax.Precision.HIGHEST, preferred_element_type=jnp.float32
    )
    energy_curves = summed.reshape(quantity_labels, 3, wave_count).transpose(1, 0, 2)
    skill_means = lax.psum(skill_terms, ("lat", "lon")) / (lon_total * weight_total)
    rms_error = jnp.sqrt(skill_means[0])
    anomaly_corr = skill_means[1] / jnp.sqrt(
        (skill_means[2] + epsilon) * (skill_means[3] + epsilon)
    )
    return (energy_curves, rms_error, anomaly_corr)


def split_np(values):
    hi = values.astype(jnp.bfloat16)
    lo = (values - hi.astype(np.float64)).astype(jnp.bfloat16)
    return hi, lo


def plan_constants(rows, cols, lat_devices, lon_devices):
    total = rows * lon_devices
    waves = total // 2 + 1
    depth = -(-rows // LANES) * LANES
    per_class = -(-(-(-waves // 4)) // 8) * 8
    table = np.zeros((4, 2 * per_class, depth), np.float64)
    lons = np.arange(rows)
    for r in range(4):
        k = np.arange(r, waves, 4)
        angle = 2.0 * np.pi * ((k[:, None] * lons[None, :]) % total) / total
        table[r, : len(k), :rows] = np.cos(angle)
        table[r, per_class : per_class + len(k), :rows] = np.sin(angle)
    hi, lo = split_np(table)
    lat_lines = cols // FIELDS
    lat_total = lat_lines * lat_devices
    all_weights = np.cos(np.pi * ((np.arange(lat_total) + 0.5) / lat_total - 0.5))
    scale = 1.0 / (float(total) * float(total) * all_weights.sum())
    tiles = cols // LANES
    piece = LANES // lon_devices
    slots = tiles + lon_devices
    col_of = np.full((slots, LANES), -1, np.int64)
    for t in range(tiles):
        col_of[t] = np.arange(LANES) + LANES * t
    for d in range(lon_devices):
        col_of[tiles + d, :piece] = (tiles - 1) * LANES + piece * d + np.arange(piece)
    valid = col_of >= 0
    field = np.where(valid, col_of % FIELDS, -1).astype(np.int32)
    weight = np.zeros((lat_devices, slots, LANES), np.float64)
    for a in range(lat_devices):
        weight[a] = np.where(valid, all_weights[a * lat_lines + np.maximum(col_of, 0) // FIELDS] * scale, 0.0)
    return hi, lo, field, weight.reshape(lat_devices * slots, LANES).astype(np.float32)


def kernel(
    dims, fore, true, norm, hi_hbm, lo_hbm, field_hbm, weight_hbm,
    result,
    fb, tb, nb, rx, ps, pr, stack, pbuf, acc, r0, half, r1, quart, r2, full,
    load_sem, own_sem, xs, xr, qs, qr, ss, sr, tab, field, weight,
):
    rows, cols, n_lat, n_lon, total = dims
    n_z = n_lat // 2
    lat = lax.axis_index("lat")
    lon = lax.axis_index("lon")
    core = lat % 2
    z = lat // 2
    tiles = cols // LANES
    own_tiles = tiles // n_lon
    slots = tiles + n_lon
    piece = LANES // n_lon
    depth = tab.shape[2] // 3
    per_class = tab.shape[1] // 2
    waves = total // 2 + 1
    n_rows = 3 * FIELDS + 4
    sibling = {"lat": lat + 1 - 2 * core, "lon": lon}

    flips = (lon, lon + 1 - 2 * (lon % 2), lon + 2 - 4 * (lon // 2), n_lon - 1 - lon)

    def lon_peer(p):
        return {"lat": lat, "lon": flips[p]}

    def z_peer(p):
        return {"lat": (z + p) % n_z * 2 + core, "lon": lon}

    barrier = pltpu.get_barrier_semaphore()
    peers = [sibling] + [lon_peer(p) for p in range(1, n_lon)] + [z_peer(p) for p in range(1, n_z)]
    for d in peers:
        pl.semaphore_signal(barrier, inc=1, device_id=d, device_id_type=MESH)
    sources = (fore, true)

    def tile_ref(a, t):
        return sources[a].at[:, pl.ds(pl.multiple_of(t * LANES, LANES), LANES)]

    pl.semaphore_wait(barrier, len(peers))

    sends = {}

    def send_tile(c):
        for p in ORDER:
            for a in range(2):
                dest = flips[p]
                sends[a, c, p] = pltpu.make_async_remote_copy(
                    src_ref=tile_ref(a, dest * own_tiles + c),
                    dst_ref=rx.at[a, c, lon],
                    send_sem=xs.at[a, c, p - 1],
                    recv_sem=xr.at[a, c, p - 1],
                    device_id=lon_peer(p),
                    device_id_type=MESH,
                )
                sends[a, c, p].start()

    send_tile(0)
    send_tile(1)
    loads = [
        pltpu.make_async_copy(src, dst, load_sem.at[i])
        for i, (src, dst) in enumerate((
            (fore, fb), (true, tb), (norm, nb), (field_hbm, field), (weight_hbm, weight),
            (hi_hbm, tab.at[:, :, :depth]), (hi_hbm, tab.at[:, :, depth : 2 * depth]), (lo_hbm, tab.at[:, :, 2 * depth :]),
        ))
    ]
    for c in loads:
        c.start()
    own = {}
    for c in range(own_tiles):
        for a in range(2):
            own[a, c] = pltpu.make_async_copy(
                tile_ref(a, lon * own_tiles + c), rx.at[a, c, lon], own_sem.at[a, c]
            )
            own[a, c].start()
    loads[0].wait()
    loads[1].wait()
    last = (tiles - 1) * LANES
    pad = jnp.zeros((depth - rows, LANES), jnp.float32)
    for a, block in enumerate((fb, tb)):
        flipped = jnp.concatenate([block[:, last : last + LANES], pad], axis=0).T
        ps[a] = flipped.reshape(n_lon, piece, depth)
    for p in ORDER:
        for a in range(2):
            sends[a, "piece", p] = pltpu.make_async_remote_copy(
                src_ref=ps.at[a, flips[p]],
                dst_ref=pr.at[a, lon],
                send_sem=qs.at[a, p - 1],
                recv_sem=qr.at[a, p - 1],
                device_id=lon_peer(p),
                device_id_type=MESH,
            )
            sends[a, "piece", p].start()
    for c in range(2, own_tiles):
        send_tile(c)

    acc[...] = jnp.zeros_like(acc)
    pbuf[...] = jnp.zeros_like(pbuf)
    for c in loads[2:5]:
        c.wait()
    field_rows = lax.broadcasted_iota(jnp.int32, (LANES, LANES), 0)

    def skill_tile(t, carry):
        lanes = pl.ds(pl.multiple_of(t * LANES, LANES), LANES)
        f, v, n = fb[:, lanes], tb[:, lanes], nb[:, lanes]
        e, af, at = f - v, f - n, v - n

        def total_of(u):
            return jnp.sum(u, axis=0, keepdims=True)

        sums = jnp.concatenate(
            [jnp.zeros((4, LANES), jnp.float32), total_of(e * e), total_of(af * at), total_of(af * af), total_of(at * at)],
            axis=0,
        )
        sums = sums * (weight[pl.ds(lat * slots + t, 1), :] * float(total))
        pick = (field_rows == field[pl.ds(t, 1), :]).astype(jnp.float32)
        return carry + lax.dot_general(
            sums, pick, (((1,), (1,)), ((), ())),
            precision=lax.Precision.HIGHEST, preferred_element_type=jnp.float32,
        )

    skill_sums = lax.fori_loop(0, tiles, skill_tile, jnp.zeros((8, LANES), jnp.float32))
    acc[n_rows - 8 : n_rows, :] = skill_sums

    out_rows = lax.broadcasted_iota(jnp.int32, (n_rows, LANES), 0)

    def put(group, a, y):
        y = jnp.concatenate([y, pad], axis=0)
        hi = y.astype(jnp.bfloat16)
        lo = (y - hi.astype(jnp.float32)).astype(jnp.bfloat16)
        at = group * 2 * LANES + a * LANES
        stack[:depth, at : at + LANES] = hi
        stack[depth : 2 * depth, at : at + LANES] = lo
        stack[2 * depth :, at : at + LANES] = hi

    def product(r, start, width):
        return jnp.dot(tab[r], stack[:, start : start + width], preferred_element_type=jnp.float32)

    def process(c, slot):
        for a in range(2):
            x = [rx[a, c, q] for q in range(4)]
            s02, s13 = x[0] + x[2], x[1] + x[3]
            put(0, a, s02 + s13)
            put(1, a, s02 - s13)
            put(2, a, x[0] - x[2])
            put(3, a, x[1] - x[3])
        w = weight[pl.ds(lat * slots + slot, 1), :]
        for r in range(4):
            if r % 2 == 0:
                both = product(r, (r // 2) * 2 * LANES, 2 * LANES)
                re, im = both[:per_class], both[per_class:]
            else:
                both = product(r, 4 * LANES, 4 * LANES)
                u, v = both[:per_class], both[per_class:]
                g = 1.0 if r == 1 else -1.0
                re = u[:, : 2 * LANES] - g * v[:, 2 * LANES :]
                im = v[:, : 2 * LANES] + g * u[:, 2 * LANES :]
            for curve in range(3):
                if curve == 2:
                    a, b = re[:, :LANES] - re[:, LANES:], im[:, :LANES] - im[:, LANES:]
                else:
                    cut = slice(curve * LANES, (curve + 1) * LANES)
                    a, b = re[:, cut], im[:, cut]
                pbuf.at[curve][pl.ds(r, per_class, stride=4), :] = (a * a + b * b) * w
        fld = field[pl.ds(slot, 1), :]
        for curve in range(3):
            power = pbuf[curve]
            hi = power.astype(jnp.bfloat16)
            lo = (power - hi.astype(jnp.float32)).astype(jnp.bfloat16)
            pick = (out_rows == jnp.where(fld >= 0, fld + FIELDS * curve, -1)).astype(jnp.float32).astype(jnp.bfloat16)
            part = lax.dot_general(
                jnp.concatenate([pick, pick], axis=1), jnp.concatenate([hi, lo], axis=1),
                (((1,), (1,)), ((), ())), preferred_element_type=jnp.float32,
            )
            for t in range(part.shape[1] // LANES):
                acc[t * n_rows : (t + 1) * n_rows, :] += part[:, t * LANES : (t + 1) * LANES]

    def take_tile(c):
        for a in range(2):
            own[a, c].wait()
            for p in range(1, n_lon):
                sends[a, c, p].wait_recv()
        process(c, lon * own_tiles + c)

    def take_piece():
        for a in range(2):
            for p in range(1, n_lon):
                sends[a, "piece", p].wait_recv()
        gap = jnp.zeros((LANES - piece, depth), jnp.float32)
        for a in range(2):
            pr[a, lon] = ps[a, lon]
            for q in range(n_lon):
                rx[a, own_tiles, q] = jnp.concatenate([pr[a, q], gap], axis=0).T[:rows]
        process(own_tiles, tiles + lon)

    for c in loads[5:]:
        c.wait()
    take_tile(0)
    take_tile(1)
    take_piece()
    for c in range(2, own_tiles):
        take_tile(c)

    size = acc.shape[0]
    s_half, s_quart = size // 2, size // (2 * n_lon)
    s_piece = s_quart // n_z

    def exchange(index, src, dst, device):
        copy = pltpu.make_async_remote_copy(
            src_ref=src, dst_ref=dst, send_sem=ss.at[index], recv_sem=sr.at[index],
            device_id=device, device_id_type=MESH,
        )
        copy.start()
        return copy

    def part(start, length):
        return pl.ds(pl.multiple_of(start, 8), length)

    def quarter(j):
        return flips[j] * s_quart

    near_first, far_first = (1, 2, 3), (3, 1, 2)
    z_order = (2, 1, 3, 0)
    cross = {
        j: exchange(
            j, acc.at[part((1 - core) * s_half + quarter(j), s_quart)],
            r0.at[part(quarter(j), s_quart)], sibling,
        )
        for j in (*far_first, 0)
    }
    base = n_lon
    over_lon = {}
    for j in (*far_first, 0):
        cross[j].wait_recv()
        rows_j = part(quarter(j), s_quart)
        half[rows_j, :] = acc[part(core * s_half + quarter(j), s_quart), :] + r0[rows_j, :]
        if j > 0:
            for p in z_order:
                at = (z + p) % n_z * s_piece
                over_lon[j, p] = exchange(
                    base + (j - 1) * n_z + p, half.at[part(quarter(j) + at, s_piece)],
                    r1.at[j - 1, part(at, s_piece)], lon_peer(j),
                )
    base += (n_lon - 1) * n_z
    over_z = {}
    for p in z_order:
        for j in range(1, n_lon):
            over_lon[j, p].wait_recv()
        at = (z + p) % n_z * s_piece
        rows_p = part(at, s_piece)
        quart[rows_p, :] = (
            half[part(quarter(0) + at, s_piece), :] + r1[0, rows_p, :] + r1[1, rows_p, :] + r1[2, rows_p, :]
        )
        if p > 0:
            over_z[p] = exchange(base + p - 1, quart.at[rows_p], r2.at[p - 1], z_peer(p))
    base += n_z - 1
    done = quart[part(z * s_piece, s_piece), :]
    for p in range(1, n_z):
        over_z[p].wait_recv()
        done = done + r2[p - 1]
    quarter_at = core * s_half + quarter(0)
    mine = part(quarter_at + z * s_piece, s_piece)
    full[mine, :] = done

    back_z = {p: exchange(base + p - 1, full.at[mine], full.at[mine], z_peer(p)) for p in (2, 1, 3)}
    base += n_z - 1
    back_lon = {}
    for p in (0, 1, 3, 2):
        if p > 0:
            back_z[p].wait_recv()
        rows_p = part(quarter_at + (z + n_z - p) % n_z * s_piece, s_piece)
        for j in far_first:
            back_lon[j, p] = exchange(base + (j - 1) * n_z + p, full.at[rows_p], full.at[rows_p], lon_peer(j))
    base += (n_lon - 1) * n_z
    back_core = {}
    for j in (0, *near_first):
        if j > 0:
            for p in range(n_z):
                back_lon[j, p].wait_recv()
        rows_j = part(core * s_half + quarter(j), s_quart)
        back_core[j] = exchange(base + j, full.at[rows_j], full.at[rows_j], sibling)
    for c in back_core.values():
        c.wait_recv()
    for group in (cross, over_lon, over_z, back_z, back_lon, back_core):
        for c in group.values():
            c.wait_send()
    for c in sends.values():
        c.wait_send()

    result[...] = full[...]


def finish(waves, full, energy, rms, corr):
    n_rows = 3 * FIELDS + 4
    for t in range(-(-waves // LANES)):
        width = min(LANES, waves - t * LANES)
        for curve in range(3):
            at = t * n_rows + curve * FIELDS
            energy[curve, :, t * LANES : t * LANES + width] = full[at : at + FIELDS, :width]
    means = full[n_rows - 4 : n_rows, :]
    m_ee, m_ft, m_ff, m_tt = means[0:1], means[1:2], means[2:3], means[3:4]
    rms[...] = jnp.sqrt(m_ee)[0, :FIELDS]
    corr[...] = (m_ft / jnp.sqrt((m_ff + epsilon) * (m_tt + epsilon)))[0, :FIELDS]


def fused(lat_devices, lon_devices, predicted_state, verified_state, normal_state):
    rows, cols = predicted_state.shape
    total = rows * lon_devices
    waves = total // 2 + 1
    tab_hi, tab_lo, field, weight = plan_constants(rows, cols, lat_devices, lon_devices)
    depth = tab_hi.shape[2]
    per_class = tab_hi.shape[1] // 2
    tiles = cols // LANES
    own_tiles = tiles // lon_devices
    piece = LANES // lon_devices
    spread = -(-4 * per_class // LANES) * LANES
    n_rows = 3 * FIELDS + 4
    n_z = lat_devices // 2
    unit = 8 * lat_devices * lon_devices
    size = -(-(spread // LANES) * n_rows // unit) * unit
    f32, b16 = jnp.float32, jnp.bfloat16
    copies = 2 * (lon_devices + lon_devices * n_z)
    dma = pltpu.SemaphoreType.DMA
    scratch = [
        pltpu.VMEM((rows, cols), f32), pltpu.VMEM((rows, cols), f32), pltpu.VMEM((rows, cols), f32),
        pltpu.VMEM((2, own_tiles + 1, lon_devices, rows, LANES), f32),
        pltpu.VMEM((2, lon_devices, piece, depth), f32),
        pltpu.VMEM((2, lon_devices, piece, depth), f32),
        pltpu.VMEM((3 * depth, 8 * LANES), b16),
        pltpu.VMEM((3, spread, LANES), f32),
        pltpu.VMEM((size, LANES), f32),
        pltpu.VMEM((size // 2, LANES), f32), pltpu.VMEM((size // 2, LANES), f32),
        pltpu.VMEM((lon_devices - 1, size // (2 * lon_devices), LANES), f32),
        pltpu.VMEM((size // (2 * lon_devices), LANES), f32),
        pltpu.VMEM((n_z - 1, size // (2 * lon_devices * n_z), LANES), f32),
        pltpu.VMEM((size, LANES), f32),
        dma((8,)), dma((2, own_tiles)),
        dma((2, own_tiles, lon_devices - 1)), dma((2, own_tiles, lon_devices - 1)),
        dma((2, lon_devices - 1)), dma((2, lon_devices - 1)),
        dma((copies,)), dma((copies,)),
        pltpu.VMEM((4, 2 * per_class, 3 * depth), b16),
        pltpu.VMEM(field.shape, jnp.int32), pltpu.VMEM(weight.shape, f32),
    ]
    any_spec = pl.BlockSpec(memory_space=pl.ANY)
    vmem = pl.BlockSpec(memory_space=pltpu.VMEM)
    dims = (rows, cols, lat_devices, lon_devices, total)
    summed = pl.pallas_call(
        functools.partial(kernel, dims),
        out_shape=jax.ShapeDtypeStruct((size, LANES), f32),
        in_specs=[any_spec] * 7,
        out_specs=vmem,
        scratch_shapes=scratch,
        compiler_params=pltpu.CompilerParams(
            collective_id=0, has_side_effects=True, vmem_limit_bytes=60_000_000
        ),
    )(predicted_state, verified_state, normal_state, jnp.asarray(tab_hi), jnp.asarray(tab_lo), jnp.asarray(field), jnp.asarray(weight))
    return pl.pallas_call(
        functools.partial(finish, waves),
        out_shape=(
            jax.ShapeDtypeStruct((3, FIELDS, waves), f32),
            jax.ShapeDtypeStruct((FIELDS,), f32),
            jax.ShapeDtypeStruct((FIELDS,), f32),
        ),
        in_specs=[vmem],
        out_specs=(vmem, vmem, vmem),
    )(summed)


def solution(mesh):
    in_specs = (P("lon", "lat"), P("lon", "lat"), P("lon", "lat"))
    out_specs = (P(), P(), P())
    n_lat, n_lon = mesh.shape["lat"], mesh.shape["lon"]

    def body(predicted_state, verified_state, normal_state):
        rows, cols = predicted_state.shape
        fits = (
            n_lon == 4 and n_lat % 2 == 0 and n_lat > 2 and rows % 8 == 0
            and cols % LANES == 0 and cols // LANES % n_lon == 1 and cols // LANES // n_lon >= 2
        )
        if fits:
            return fused(n_lat, n_lon, predicted_state, verified_state, normal_state)
        return local(predicted_state, verified_state, normal_state)

    return jax.shard_map(body, mesh=mesh, in_specs=in_specs, out_specs=out_specs, check_vma=False)
```

```python
import functools

import jax
import jax.numpy as jnp
import numpy as np
from jax import lax
from jax.experimental import pallas as pl
from jax.experimental.pallas import tpu as pltpu
from jax.sharding import PartitionSpec as P

FIELDS = 52
LANES = 128
MESH = pl.DeviceIdType.MESH
ORDER = (3, 1, 2)


epsilon = 1e-06


def latitude_weights(lat_index, parallel_number):
    return jnp.cos(jnp.pi * ((lat_index.astype(jnp.float32) + 0.5) / parallel_number - 0.5))


def dft_table(lon_rows, lon_total, wave_count):
    longitudes = jnp.arange(lon_rows, dtype=jnp.int32)
    waves = jnp.arange(wave_count, dtype=jnp.int32)
    phase = longitudes[:, None] * waves[None, :] % lon_total
    angle = 2.0 * jnp.pi / lon_total * phase.astype(jnp.float32)
    return jnp.concatenate([jnp.cos(angle), -jnp.sin(angle)], axis=1)


def transform_columns(stacked, table):
    return lax.dot_general(
        stacked,
        table,
        (((0,), (0,)), ((), ())),
        precision=lax.Precision.HIGHEST,
        preferred_element_type=jnp.float32,
    )


def row_powers(fore_coeffs, true_coeffs, wave_count):
    diff_coeffs = fore_coeffs - true_coeffs

    def square(coeffs):
        return (
            coeffs[:, :wave_count] * coeffs[:, :wave_count]
            + coeffs[:, wave_count:] * coeffs[:, wave_count:]
        )

    return jnp.stack([square(fore_coeffs), square(true_coeffs), square(diff_coeffs)], axis=1)


def local(predicted_state, verified_state, normal_state):
    quantity_labels = FIELDS
    meridian_lines, meridian_number = predicted_state.shape
    parallel_lines = meridian_number // quantity_labels
    parallel_number = parallel_lines * lax.axis_size("lat")
    lon_devices = lax.axis_size("lon")
    lon_total = meridian_lines * lon_devices
    wave_count = lon_total // 2 + 1
    row_share = meridian_number // lon_devices
    lat_first = lax.axis_index("lat") * parallel_lines
    weights = latitude_weights(
        lat_first + jnp.arange(parallel_lines, dtype=jnp.int32), parallel_number
    )
    weight_total = jnp.sum(
        latitude_weights(jnp.arange(parallel_number, dtype=jnp.int32), parallel_number)
    )
    predicted_block = predicted_state.reshape(meridian_lines, parallel_lines, quantity_labels)
    observed_block = verified_state.reshape(meridian_lines, parallel_lines, quantity_labels)
    normal_block = normal_state.reshape(meridian_lines, parallel_lines, quantity_labels)
    mismatch_parts = predicted_block - observed_block
    predicted_anomalies = predicted_block - normal_block
    observed_anomalies = observed_block - normal_block
    broad_layout = weights[None, :, None]
    skill_terms = jnp.stack(
        [
            jnp.sum(broad_layout * mismatch_parts * mismatch_parts, axis=(0, 1)),
            jnp.sum(broad_layout * predicted_anomalies * observed_anomalies, axis=(0, 1)),
            jnp.sum(broad_layout * predicted_anomalies * predicted_anomalies, axis=(0, 1)),
            jnp.sum(broad_layout * observed_anomalies * observed_anomalies, axis=(0, 1)),
        ]
    )
    predicted_meridians = predicted_block.transpose(0, 2, 1).reshape(
        meridian_lines, meridian_number
    )
    true_cols = observed_block.transpose(0, 2, 1).reshape(meridian_lines, meridian_number)
    full_table = dft_table(lon_total, lon_total, wave_count)
    fore_blocks = predicted_meridians.reshape(meridian_lines, lon_devices, row_share)
    true_blocks = true_cols.reshape(meridian_lines, lon_devices, row_share)
    fore_part = lax.all_to_all(fore_blocks, "lon", split_axis=1, concat_axis=0, tiled=True)[:, 0, :]
    true_part = lax.all_to_all(true_blocks, "lon", split_axis=1, concat_axis=0, tiled=True)[:, 0, :]
    items = fore_part.shape[1]
    stacked = jnp.concatenate([fore_part, true_part], axis=1)
    coeffs = transform_columns(stacked, full_table)
    powers = row_powers(coeffs[:items], coeffs[items:], wave_count)
    share_start = lax.axis_index("lon") * row_share
    global_cols = share_start + jnp.arange(row_share, dtype=jnp.int32)
    field_of = global_cols // parallel_lines
    row_weights = latitude_weights(lat_first + global_cols % parallel_lines, parallel_number)
    row_scale = row_weights / (lon_total * lon_total * weight_total)
    weighted = powers.reshape(row_share, 3 * wave_count) * row_scale[:, None]
    field_index = jnp.arange(quantity_labels, dtype=jnp.int32)
    window = min(quantity_labels, row_share // parallel_lines + 2)
    first_field = share_start // parallel_lines
    window_index = jnp.arange(window, dtype=jnp.int32)
    offset = field_of - first_field
    selector = (offset[None, :] == window_index[:, None]).astype(jnp.float32)
    band_sum = jnp.dot(
        selector, weighted, precision=lax.Precision.HIGHEST, preferred_element_type=jnp.float32
    )
    band_sum = lax.psum(band_sum, "lat")
    gathered = lax.all_gather(band_sum, "lon", axis=0, tiled=True)
    slot_index = jnp.arange(lon_devices * window, dtype=jnp.int32)
    slot_field = slot_index // window * row_share // parallel_lines + slot_index % window
    placer = (slot_field[None, :] == field_index[:, None]).astype(jnp.float32)
    summed = jnp.dot(
        placer, gathered, precision=lax.Precision.HIGHEST, preferred_element_type=jnp.float32
    )
    energy_curves = summed.reshape(quantity_labels, 3, wave_count).transpose(1, 0, 2)
    skill_means = lax.psum(skill_terms, ("lat", "lon")) / (lon_total * weight_total)
    rms_error = jnp.sqrt(skill_means[0])
    anomaly_corr = skill_means[1] / jnp.sqrt(
        (skill_means[2] + epsilon) * (skill_means[3] + epsilon)
    )
    return (energy_curves, rms_error, anomaly_corr)


def split_np(values):
    hi = values.astype(jnp.bfloat16)
    lo = (values - hi.astype(np.float64)).astype(jnp.bfloat16)
    return hi, lo


def plan_constants(rows, cols, lat_devices, lon_devices):
    total = rows * lon_devices
    waves = total // 2 + 1
    depth = -(-rows // LANES) * LANES
    per_class = -(-(-(-waves // 4)) // 8) * 8
    table = np.zeros((4, 2 * per_class, depth), np.float64)
    lons = np.arange(rows)
    for r in range(4):
        k = np.arange(r, waves, 4)
        angle = 2.0 * np.pi * ((k[:, None] * lons[None, :]) % total) / total
        table[r, : len(k), :rows] = np.cos(angle)
        table[r, per_class : per_class + len(k), :rows] = np.sin(angle)
    hi, lo = split_np(table)
    lat_lines = cols // FIELDS
    lat_total = lat_lines * lat_devices
    all_weights = np.cos(np.pi * ((np.arange(lat_total) + 0.5) / lat_total - 0.5))
    scale = 1.0 / (float(total) * float(total) * all_weights.sum())
    tiles = cols // LANES
    piece = LANES // lon_devices
    slots = tiles + lon_devices
    col_of = np.full((slots, LANES), -1, np.int64)
    for t in range(tiles):
        col_of[t] = np.arange(LANES) + LANES * t
    for d in range(lon_devices):
        col_of[tiles + d, :piece] = (tiles - 1) * LANES + piece * d + np.arange(piece)
    valid = col_of >= 0
    field = np.where(valid, col_of % FIELDS, -1).astype(np.int32)
    weight = np.zeros((lat_devices, slots, LANES), np.float64)
    for a in range(lat_devices):
        weight[a] = np.where(valid, all_weights[a * lat_lines + np.maximum(col_of, 0) // FIELDS] * scale, 0.0)
    return hi, lo, field, weight.reshape(lat_devices * slots, LANES).astype(np.float32)


def kernel(
    dims, fore, true, norm, hi_hbm, lo_hbm, field_hbm, weight_hbm,
    result,
    fb, tb, nb, rx, ps, pr, stack, pbuf, acc, r0, half, r1, r2, full,
    load_sem, own_sem, xs, xr, qs, qr, ss, sr, tab, field, weight,
):
    rows, cols, n_lat, n_lon, total = dims
    n_z = n_lat // 2
    lat = lax.axis_index("lat")
    lon = lax.axis_index("lon")
    core = lat % 2
    z = lat // 2
    tiles = cols // LANES
    own_tiles = tiles // n_lon
    slots = tiles + n_lon
    piece = LANES // n_lon
    depth = tab.shape[2] // 3
    per_class = tab.shape[1] // 2
    waves = total // 2 + 1
    n_rows = 3 * FIELDS + 4
    sibling = {"lat": lat + 1 - 2 * core, "lon": lon}

    flips = (lon, lon + 1 - 2 * (lon % 2), lon + 2 - 4 * (lon // 2), n_lon - 1 - lon)

    def lon_peer(p):
        return {"lat": lat, "lon": flips[p]}

    def z_peer(p):
        return {"lat": (z + p) % n_z * 2 + core, "lon": lon}

    barrier = pltpu.get_barrier_semaphore()
    peers = [sibling] + [lon_peer(p) for p in range(1, n_lon)] + [z_peer(p) for p in range(1, n_z)]
    for d in peers:
        pl.semaphore_signal(barrier, inc=1, device_id=d, device_id_type=MESH)
    sources = (fore, true)

    def tile_ref(a, t):
        return sources[a].at[:, pl.ds(pl.multiple_of(t * LANES, LANES), LANES)]

    pl.semaphore_wait(barrier, len(peers))

    sends = {}

    def send_tile(c):
        for p in ORDER:
            for a in range(2):
                dest = flips[p]
                sends[a, c, p] = pltpu.make_async_remote_copy(
                    src_ref=tile_ref(a, dest * own_tiles + c),
                    dst_ref=rx.at[a, c, lon],
                    send_sem=xs.at[a, c, p - 1],
                    recv_sem=xr.at[a, c, p - 1],
                    device_id=lon_peer(p),
                    device_id_type=MESH,
                )
                sends[a, c, p].start()

    send_tile(0)
    send_tile(1)
    loads = [
        pltpu.make_async_copy(src, dst, load_sem.at[i])
        for i, (src, dst) in enumerate((
            (fore, fb), (true, tb), (norm, nb), (field_hbm, field), (weight_hbm, weight),
            (hi_hbm, tab.at[:, :, :depth]), (hi_hbm, tab.at[:, :, depth : 2 * depth]), (lo_hbm, tab.at[:, :, 2 * depth :]),
        ))
    ]
    for c in loads:
        c.start()
    own = {}
    for c in range(own_tiles):
        for a in range(2):
            own[a, c] = pltpu.make_async_copy(
                tile_ref(a, lon * own_tiles + c), rx.at[a, c, lon], own_sem.at[a, c]
            )
            own[a, c].start()
    loads[0].wait()
    loads[1].wait()
    last = (tiles - 1) * LANES
    pad = jnp.zeros((depth - rows, LANES), jnp.float32)
    for a, block in enumerate((fb, tb)):
        flipped = jnp.concatenate([block[:, last : last + LANES], pad], axis=0).T
        ps[a] = flipped.reshape(n_lon, piece, depth)
    for p in ORDER:
        for a in range(2):
            sends[a, "piece", p] = pltpu.make_async_remote_copy(
                src_ref=ps.at[a, flips[p]],
                dst_ref=pr.at[a, lon],
                send_sem=qs.at[a, p - 1],
                recv_sem=qr.at[a, p - 1],
                device_id=lon_peer(p),
                device_id_type=MESH,
            )
            sends[a, "piece", p].start()
    for c in range(2, own_tiles):
        send_tile(c)

    acc[...] = jnp.zeros_like(acc)
    pbuf[...] = jnp.zeros_like(pbuf)
    for c in loads[2:5]:
        c.wait()
    field_rows = lax.broadcasted_iota(jnp.int32, (LANES, LANES), 0)

    def skill_tile(t, carry):
        lanes = pl.ds(pl.multiple_of(t * LANES, LANES), LANES)
        f, v, n = fb[:, lanes], tb[:, lanes], nb[:, lanes]
        e, af, at = f - v, f - n, v - n

        def total_of(u):
            return jnp.sum(u, axis=0, keepdims=True)

        sums = jnp.concatenate(
            [jnp.zeros((4, LANES), jnp.float32), total_of(e * e), total_of(af * at), total_of(af * af), total_of(at * at)],
            axis=0,
        )
        sums = sums * (weight[pl.ds(lat * slots + t, 1), :] * float(total))
        pick = (field_rows == field[pl.ds(t, 1), :]).astype(jnp.float32)
        return carry + lax.dot_general(
            sums, pick, (((1,), (1,)), ((), ())),
            precision=lax.Precision.HIGHEST, preferred_element_type=jnp.float32,
        )

    skill_sums = lax.fori_loop(0, tiles, skill_tile, jnp.zeros((8, LANES), jnp.float32))
    acc[n_rows - 8 : n_rows, :] = skill_sums

    out_rows = lax.broadcasted_iota(jnp.int32, (n_rows, LANES), 0)

    def put(group, a, y):
        y = jnp.concatenate([y, pad], axis=0)
        hi = y.astype(jnp.bfloat16)
        lo = (y - hi.astype(jnp.float32)).astype(jnp.bfloat16)
        at = group * 2 * LANES + a * LANES
        stack[:depth, at : at + LANES] = hi
        stack[depth : 2 * depth, at : at + LANES] = lo
        stack[2 * depth :, at : at + LANES] = hi

    def product(r, start, width):
        return jnp.dot(tab[r], stack[:, start : start + width], preferred_element_type=jnp.float32)

    def process(c, slot):
        for a in range(2):
            x = [rx[a, c, q] for q in range(4)]
            s02, s13 = x[0] + x[2], x[1] + x[3]
            put(0, a, s02 + s13)
            put(1, a, s02 - s13)
            put(2, a, x[0] - x[2])
            put(3, a, x[1] - x[3])
        w = weight[pl.ds(lat * slots + slot, 1), :]
        for r in range(4):
            if r % 2 == 0:
                both = product(r, (r // 2) * 2 * LANES, 2 * LANES)
                re, im = both[:per_class], both[per_class:]
            else:
                both = product(r, 4 * LANES, 4 * LANES)
                u, v = both[:per_class], both[per_class:]
                g = 1.0 if r == 1 else -1.0
                re = u[:, : 2 * LANES] - g * v[:, 2 * LANES :]
                im = v[:, : 2 * LANES] + g * u[:, 2 * LANES :]
            for curve in range(3):
                if curve == 2:
                    a, b = re[:, :LANES] - re[:, LANES:], im[:, :LANES] - im[:, LANES:]
                else:
                    cut = slice(curve * LANES, (curve + 1) * LANES)
                    a, b = re[:, cut], im[:, cut]
                pbuf.at[curve][pl.ds(r, per_class, stride=4), :] = (a * a + b * b) * w
        fld = field[pl.ds(slot, 1), :]
        for curve in range(3):
            power = pbuf[curve]
            hi = power.astype(jnp.bfloat16)
            lo = (power - hi.astype(jnp.float32)).astype(jnp.bfloat16)
            pick = (out_rows == jnp.where(fld >= 0, fld + FIELDS * curve, -1)).astype(jnp.float32).astype(jnp.bfloat16)
            part = lax.dot_general(
                jnp.concatenate([pick, pick], axis=1), jnp.concatenate([hi, lo], axis=1),
                (((1,), (1,)), ((), ())), preferred_element_type=jnp.float32,
            )
            for t in range(part.shape[1] // LANES):
                acc[t * n_rows : (t + 1) * n_rows, :] += part[:, t * LANES : (t + 1) * LANES]

    def take_tile(c):
        for a in range(2):
            own[a, c].wait()
            for p in range(1, n_lon):
                sends[a, c, p].wait_recv()
        process(c, lon * own_tiles + c)

    def take_piece():
        for a in range(2):
            for p in range(1, n_lon):
                sends[a, "piece", p].wait_recv()
        gap = jnp.zeros((LANES - piece, depth), jnp.float32)
        for a in range(2):
            pr[a, lon] = ps[a, lon]
            for q in range(n_lon):
                rx[a, own_tiles, q] = jnp.concatenate([pr[a, q], gap], axis=0).T[:rows]
        process(own_tiles, tiles + lon)

    for c in loads[5:]:
        c.wait()
    take_tile(0)
    take_tile(1)
    take_piece()
    for c in range(2, own_tiles):
        take_tile(c)

    size = acc.shape[0]
    s_half, s_quart = size // 2, size // (2 * n_lon)
    s_piece = s_quart // n_z

    def exchange(index, src, dst, device):
        copy = pltpu.make_async_remote_copy(
            src_ref=src, dst_ref=dst, send_sem=ss.at[index], recv_sem=sr.at[index],
            device_id=device, device_id_type=MESH,
        )
        copy.start()
        return copy

    def part(start, length):
        return pl.ds(pl.multiple_of(start, 8), length)

    def quarter(j):
        return flips[j] * s_quart

    near_first, far_first = (1, 2, 3), (3, 1, 2)
    cross = {
        j: exchange(
            j, acc.at[part((1 - core) * s_half + quarter(j), s_quart)],
            r0.at[part(quarter(j), s_quart)], sibling,
        )
        for j in (*far_first, 0)
    }
    base = n_lon
    over_lon = {}
    for j in (*far_first, 0):
        cross[j].wait_recv()
        rows_j = part(quarter(j), s_quart)
        half[rows_j, :] = acc[part(core * s_half + quarter(j), s_quart), :] + r0[rows_j, :]
        if j > 0:
            for p in range(n_z):
                at = p * s_piece
                over_lon[j, p] = exchange(
                    base + (j - 1) * n_z + p, half.at[part(quarter(j) + at, s_piece)],
                    r1.at[j - 1, part(at, s_piece)], lon_peer(j),
                )
    base += (n_lon - 1) * n_z
    over_z = {}
    z_order = (2, 1, 3)
    for s in range(n_z):
        for j in range(1, n_lon):
            over_lon[j, s].wait_recv()
        rows_s = pl.ds(s * s_piece, s_piece)
        r2[z, rows_s, :] = (
            half[part(quarter(0) + s * s_piece, s_piece), :] + r1[0, rows_s, :] + r1[1, rows_s, :] + r1[2, rows_s, :]
        )
        for p in z_order:
            over_z[p, s] = exchange(base + (p - 1) * n_z + s, r2.at[z, rows_s], r2.at[z, rows_s], z_peer(p))
    base += (n_z - 1) * n_z
    quarter_at = core * s_half + quarter(0)
    back_lon = {}
    for s in range(n_z):
        for p in z_order:
            over_z[p, s].wait_recv()
        rows_s = pl.ds(s * s_piece, s_piece)
        mine = part(quarter_at + s * s_piece, s_piece)
        full[mine, :] = r2[0, rows_s, :] + r2[1, rows_s, :] + r2[2, rows_s, :] + r2[3, rows_s, :]
        for j in far_first:
            back_lon[j, s] = exchange(base + (j - 1) * n_z + s, full.at[mine], full.at[mine], lon_peer(j))
    base += (n_lon - 1) * n_z
    back_core = {}
    for j in (0, *near_first):
        if j > 0:
            for p in range(n_z):
                back_lon[j, p].wait_recv()
        rows_j = part(core * s_half + quarter(j), s_quart)
        back_core[j] = exchange(base + j, full.at[rows_j], full.at[rows_j], sibling)
    for c in back_core.values():
        c.wait_recv()
    for group in (cross, over_lon, over_z, back_lon, back_core):
        for c in group.values():
            c.wait_send()
    for c in sends.values():
        c.wait_send()

    result[...] = full[...]


def finish(waves, full, energy, rms, corr):
    n_rows = 3 * FIELDS + 4
    for t in range(-(-waves // LANES)):
        width = min(LANES, waves - t * LANES)
        for curve in range(3):
            at = t * n_rows + curve * FIELDS
            energy[curve, :, t * LANES : t * LANES + width] = full[at : at + FIELDS, :width]
    means = full[n_rows - 4 : n_rows, :]
    m_ee, m_ft, m_ff, m_tt = means[0:1], means[1:2], means[2:3], means[3:4]
    rms[...] = jnp.sqrt(m_ee)[0, :FIELDS]
    corr[...] = (m_ft / jnp.sqrt((m_ff + epsilon) * (m_tt + epsilon)))[0, :FIELDS]


def fused(lat_devices, lon_devices, predicted_state, verified_state, normal_state):
    rows, cols = predicted_state.shape
    total = rows * lon_devices
    waves = total // 2 + 1
    tab_hi, tab_lo, field, weight = plan_constants(rows, cols, lat_devices, lon_devices)
    depth = tab_hi.shape[2]
    per_class = tab_hi.shape[1] // 2
    tiles = cols // LANES
    own_tiles = tiles // lon_devices
    piece = LANES // lon_devices
    spread = -(-4 * per_class // LANES) * LANES
    n_rows = 3 * FIELDS + 4
    n_z = lat_devices // 2
    unit = 8 * lat_devices * lon_devices
    size = -(-(spread // LANES) * n_rows // unit) * unit
    f32, b16 = jnp.float32, jnp.bfloat16
    copies = 3 * lon_devices * n_z
    dma = pltpu.SemaphoreType.DMA
    scratch = [
        pltpu.VMEM((rows, cols), f32), pltpu.VMEM((rows, cols), f32), pltpu.VMEM((rows, cols), f32),
        pltpu.VMEM((2, own_tiles + 1, lon_devices, rows, LANES), f32),
        pltpu.VMEM((2, lon_devices, piece, depth), f32),
        pltpu.VMEM((2, lon_devices, piece, depth), f32),
        pltpu.VMEM((3 * depth, 8 * LANES), b16),
        pltpu.VMEM((3, spread, LANES), f32),
        pltpu.VMEM((size, LANES), f32),
        pltpu.VMEM((size // 2, LANES), f32), pltpu.VMEM((size // 2, LANES), f32),
        pltpu.VMEM((lon_devices - 1, size // (2 * lon_devices), LANES), f32),
        pltpu.VMEM((n_z, size // (2 * lon_devices), LANES), f32),
        pltpu.VMEM((size, LANES), f32),
        dma((8,)), dma((2, own_tiles)),
        dma((2, own_tiles, lon_devices - 1)), dma((2, own_tiles, lon_devices - 1)),
        dma((2, lon_devices - 1)), dma((2, lon_devices - 1)),
        dma((copies,)), dma((copies,)),
        pltpu.VMEM((4, 2 * per_class, 3 * depth), b16),
        pltpu.VMEM(field.shape, jnp.int32), pltpu.VMEM(weight.shape, f32),
    ]
    any_spec = pl.BlockSpec(memory_space=pl.ANY)
    vmem = pl.BlockSpec(memory_space=pltpu.VMEM)
    dims = (rows, cols, lat_devices, lon_devices, total)
    summed = pl.pallas_call(
        functools.partial(kernel, dims),
        out_shape=jax.ShapeDtypeStruct((size, LANES), f32),
        in_specs=[any_spec] * 7,
        out_specs=vmem,
        scratch_shapes=scratch,
        compiler_params=pltpu.CompilerParams(
            collective_id=0, has_side_effects=True, vmem_limit_bytes=60_000_000
        ),
    )(predicted_state, verified_state, normal_state, jnp.asarray(tab_hi), jnp.asarray(tab_lo), jnp.asarray(field), jnp.asarray(weight))
    return pl.pallas_call(
        functools.partial(finish, waves),
        out_shape=(
            jax.ShapeDtypeStruct((3, FIELDS, waves), f32),
            jax.ShapeDtypeStruct((FIELDS,), f32),
            jax.ShapeDtypeStruct((FIELDS,), f32),
        ),
        in_specs=[vmem],
        out_specs=(vmem, vmem, vmem),
    )(summed)


def solution(mesh):
    in_specs = (P("lon", "lat"), P("lon", "lat"), P("lon", "lat"))
    out_specs = (P(), P(), P())
    n_lat, n_lon = mesh.shape["lat"], mesh.shape["lon"]

    def body(predicted_state, verified_state, normal_state):
        rows, cols = predicted_state.shape
        fits = (
            n_lon == 4 and n_lat == 8 and rows % 8 == 0
            and cols % LANES == 0 and cols // LANES % n_lon == 1 and cols // LANES // n_lon >= 2
        )
        if fits:
            return fused(n_lat, n_lon, predicted_state, verified_state, normal_state)
        return local(predicted_state, verified_state, normal_state)

    return jax.shard_map(body, mesh=mesh, in_specs=in_specs, out_specs=out_specs, check_vma=False)
```

```python
import functools

import jax
import jax.numpy as jnp
import numpy as np
from jax import lax
from jax.experimental import pallas as pl
from jax.experimental.pallas import tpu as pltpu
from jax.sharding import PartitionSpec as P

FIELDS = 52
LANES = 128
MESH = pl.DeviceIdType.MESH
ORDER = (3, 1, 2)


epsilon = 1e-06


def latitude_weights(lat_index, parallel_number):
    return jnp.cos(jnp.pi * ((lat_index.astype(jnp.float32) + 0.5) / parallel_number - 0.5))


def dft_table(lon_rows, lon_total, wave_count):
    longitudes = jnp.arange(lon_rows, dtype=jnp.int32)
    waves = jnp.arange(wave_count, dtype=jnp.int32)
    phase = longitudes[:, None] * waves[None, :] % lon_total
    angle = 2.0 * jnp.pi / lon_total * phase.astype(jnp.float32)
    return jnp.concatenate([jnp.cos(angle), -jnp.sin(angle)], axis=1)


def transform_columns(stacked, table):
    return lax.dot_general(
        stacked,
        table,
        (((0,), (0,)), ((), ())),
        precision=lax.Precision.HIGHEST,
        preferred_element_type=jnp.float32,
    )


def row_powers(fore_coeffs, true_coeffs, wave_count):
    diff_coeffs = fore_coeffs - true_coeffs

    def square(coeffs):
        return (
            coeffs[:, :wave_count] * coeffs[:, :wave_count]
            + coeffs[:, wave_count:] * coeffs[:, wave_count:]
        )

    return jnp.stack([square(fore_coeffs), square(true_coeffs), square(diff_coeffs)], axis=1)


def local(predicted_state, verified_state, normal_state):
    quantity_labels = FIELDS
    meridian_lines, meridian_number = predicted_state.shape
    parallel_lines = meridian_number // quantity_labels
    parallel_number = parallel_lines * lax.axis_size("lat")
    lon_devices = lax.axis_size("lon")
    lon_total = meridian_lines * lon_devices
    wave_count = lon_total // 2 + 1
    row_share = meridian_number // lon_devices
    lat_first = lax.axis_index("lat") * parallel_lines
    weights = latitude_weights(
        lat_first + jnp.arange(parallel_lines, dtype=jnp.int32), parallel_number
    )
    weight_total = jnp.sum(
        latitude_weights(jnp.arange(parallel_number, dtype=jnp.int32), parallel_number)
    )
    predicted_block = predicted_state.reshape(meridian_lines, parallel_lines, quantity_labels)
    observed_block = verified_state.reshape(meridian_lines, parallel_lines, quantity_labels)
    normal_block = normal_state.reshape(meridian_lines, parallel_lines, quantity_labels)
    mismatch_parts = predicted_block - observed_block
    predicted_anomalies = predicted_block - normal_block
    observed_anomalies = observed_block - normal_block
    broad_layout = weights[None, :, None]
    skill_terms = jnp.stack(
        [
            jnp.sum(broad_layout * mismatch_parts * mismatch_parts, axis=(0, 1)),
            jnp.sum(broad_layout * predicted_anomalies * observed_anomalies, axis=(0, 1)),
            jnp.sum(broad_layout * predicted_anomalies * predicted_anomalies, axis=(0, 1)),
            jnp.sum(broad_layout * observed_anomalies * observed_anomalies, axis=(0, 1)),
        ]
    )
    predicted_meridians = predicted_block.transpose(0, 2, 1).reshape(
        meridian_lines, meridian_number
    )
    true_cols = observed_block.transpose(0, 2, 1).reshape(meridian_lines, meridian_number)
    full_table = dft_table(lon_total, lon_total, wave_count)
    fore_blocks = predicted_meridians.reshape(meridian_lines, lon_devices, row_share)
    true_blocks = true_cols.reshape(meridian_lines, lon_devices, row_share)
    fore_part = lax.all_to_all(fore_blocks, "lon", split_axis=1, concat_axis=0, tiled=True)[:, 0, :]
    true_part = lax.all_to_all(true_blocks, "lon", split_axis=1, concat_axis=0, tiled=True)[:, 0, :]
    items = fore_part.shape[1]
    stacked = jnp.concatenate([fore_part, true_part], axis=1)
    coeffs = transform_columns(stacked, full_table)
    powers = row_powers(coeffs[:items], coeffs[items:], wave_count)
    share_start = lax.axis_index("lon") * row_share
    global_cols = share_start + jnp.arange(row_share, dtype=jnp.int32)
    field_of = global_cols // parallel_lines
    row_weights = latitude_weights(lat_first + global_cols % parallel_lines, parallel_number)
    row_scale = row_weights / (lon_total * lon_total * weight_total)
    weighted = powers.reshape(row_share, 3 * wave_count) * row_scale[:, None]
    field_index = jnp.arange(quantity_labels, dtype=jnp.int32)
    window = min(quantity_labels, row_share // parallel_lines + 2)
    first_field = share_start // parallel_lines
    window_index = jnp.arange(window, dtype=jnp.int32)
    offset = field_of - first_field
    selector = (offset[None, :] == window_index[:, None]).astype(jnp.float32)
    band_sum = jnp.dot(
        selector, weighted, precision=lax.Precision.HIGHEST, preferred_element_type=jnp.float32
    )
    band_sum = lax.psum(band_sum, "lat")
    gathered = lax.all_gather(band_sum, "lon", axis=0, tiled=True)
    slot_index = jnp.arange(lon_devices * window, dtype=jnp.int32)
    slot_field = slot_index // window * row_share // parallel_lines + slot_index % window
    placer = (slot_field[None, :] == field_index[:, None]).astype(jnp.float32)
    summed = jnp.dot(
        placer, gathered, precision=lax.Precision.HIGHEST, preferred_element_type=jnp.float32
    )
    energy_curves = summed.reshape(quantity_labels, 3, wave_count).transpose(1, 0, 2)
    skill_means = lax.psum(skill_terms, ("lat", "lon")) / (lon_total * weight_total)
    rms_error = jnp.sqrt(skill_means[0])
    anomaly_corr = skill_means[1] / jnp.sqrt(
        (skill_means[2] + epsilon) * (skill_means[3] + epsilon)
    )
    return (energy_curves, rms_error, anomaly_corr)


def split_np(values):
    hi = values.astype(jnp.bfloat16)
    lo = (values - hi.astype(np.float64)).astype(jnp.bfloat16)
    return hi, lo


def plan_constants(rows, cols, lat_devices, lon_devices):
    total = rows * lon_devices
    waves = total // 2 + 1
    depth = -(-rows // LANES) * LANES
    per_class = -(-(-(-waves // 4)) // 8) * 8
    table = np.zeros((4, 2 * per_class, depth), np.float64)
    lons = np.arange(rows)
    for r in range(4):
        k = np.arange(r, waves, 4)
        angle = 2.0 * np.pi * ((k[:, None] * lons[None, :]) % total) / total
        table[r, : len(k), :rows] = np.cos(angle)
        table[r, per_class : per_class + len(k), :rows] = np.sin(angle)
    hi, lo = split_np(table)
    lat_lines = cols // FIELDS
    lat_total = lat_lines * lat_devices
    all_weights = np.cos(np.pi * ((np.arange(lat_total) + 0.5) / lat_total - 0.5))
    scale = 1.0 / (float(total) * float(total) * all_weights.sum())
    tiles = cols // LANES
    piece = LANES // lon_devices
    slots = tiles + lon_devices
    col_of = np.full((slots, LANES), -1, np.int64)
    for t in range(tiles):
        col_of[t] = np.arange(LANES) + LANES * t
    for d in range(lon_devices):
        col_of[tiles + d, :piece] = (tiles - 1) * LANES + piece * d + np.arange(piece)
    valid = col_of >= 0
    field = np.where(valid, col_of % FIELDS, -1).astype(np.int32)
    weight = np.zeros((lat_devices, slots, LANES), np.float64)
    for a in range(lat_devices):
        weight[a] = np.where(valid, all_weights[a * lat_lines + np.maximum(col_of, 0) // FIELDS] * scale, 0.0)
    return hi, lo, field, weight.reshape(lat_devices * slots, LANES).astype(np.float32)


def kernel(
    dims, fore, true, norm, hi_hbm, lo_hbm, field_hbm, weight_hbm,
    result,
    fb, tb, nb, rx, ps, pr, stack, pbuf, acc, r0, half, r1, r2, full,
    load_sem, own_sem, xs, xr, qs, qr, ss, sr, tab, field, weight,
):
    rows, cols, n_lat, n_lon, total = dims
    n_z = n_lat // 2
    lat = lax.axis_index("lat")
    lon = lax.axis_index("lon")
    core = lat % 2
    z = lat // 2
    tiles = cols // LANES
    own_tiles = tiles // n_lon
    slots = tiles + n_lon
    piece = LANES // n_lon
    depth = tab.shape[2] // 3
    per_class = tab.shape[1] // 2
    waves = total // 2 + 1
    n_rows = 3 * FIELDS + 4
    sibling = {"lat": lat + 1 - 2 * core, "lon": lon}

    flips = (lon, lon + 1 - 2 * (lon % 2), lon + 2 - 4 * (lon // 2), n_lon - 1 - lon)

    def lon_peer(p):
        return {"lat": lat, "lon": flips[p]}

    def z_peer(p):
        return {"lat": (z + p) % n_z * 2 + core, "lon": lon}

    barrier = pltpu.get_barrier_semaphore()
    peers = [sibling] + [lon_peer(p) for p in range(1, n_lon)] + [z_peer(p) for p in range(1, n_z)]
    for d in peers:
        pl.semaphore_signal(barrier, inc=1, device_id=d, device_id_type=MESH)
    sources = (fore, true)

    def tile_ref(a, t):
        return sources[a].at[:, pl.ds(pl.multiple_of(t * LANES, LANES), LANES)]

    pl.semaphore_wait(barrier, len(peers))

    sends = {}

    def send_tile(c):
        for p in ORDER:
            for a in range(2):
                dest = flips[p]
                sends[a, c, p] = pltpu.make_async_remote_copy(
                    src_ref=tile_ref(a, dest * own_tiles + c),
                    dst_ref=rx.at[a, c, lon],
                    send_sem=xs.at[a, c, p - 1],
                    recv_sem=xr.at[a, c, p - 1],
                    device_id=lon_peer(p),
                    device_id_type=MESH,
                )
                sends[a, c, p].start()

    send_tile(0)
    send_tile(1)
    loads = [
        pltpu.make_async_copy(src, dst, load_sem.at[i])
        for i, (src, dst) in enumerate((
            (fore, fb), (true, tb), (norm, nb), (field_hbm, field), (weight_hbm, weight),
            (hi_hbm, tab.at[:, :, :depth]), (hi_hbm, tab.at[:, :, depth : 2 * depth]), (lo_hbm, tab.at[:, :, 2 * depth :]),
        ))
    ]
    for c in loads:
        c.start()
    own = {}
    for c in range(own_tiles):
        for a in range(2):
            own[a, c] = pltpu.make_async_copy(
                tile_ref(a, lon * own_tiles + c), rx.at[a, c, lon], own_sem.at[a, c]
            )
            own[a, c].start()
    loads[0].wait()
    loads[1].wait()
    last = (tiles - 1) * LANES
    pad = jnp.zeros((depth - rows, LANES), jnp.float32)
    for a, block in enumerate((fb, tb)):
        flipped = jnp.concatenate([block[:, last : last + LANES], pad], axis=0).T
        ps[a] = flipped.reshape(n_lon, piece, depth)
    for p in ORDER:
        for a in range(2):
            sends[a, "piece", p] = pltpu.make_async_remote_copy(
                src_ref=ps.at[a, flips[p]],
                dst_ref=pr.at[a, lon],
                send_sem=qs.at[a, p - 1],
                recv_sem=qr.at[a, p - 1],
                device_id=lon_peer(p),
                device_id_type=MESH,
            )
            sends[a, "piece", p].start()
    for c in range(2, own_tiles):
        send_tile(c)

    acc[...] = jnp.zeros_like(acc)
    pbuf[...] = jnp.zeros_like(pbuf)
    for c in loads[2:5]:
        c.wait()
    field_rows = lax.broadcasted_iota(jnp.int32, (LANES, LANES), 0)

    def skill_tile(t, carry):
        lanes = pl.ds(pl.multiple_of(t * LANES, LANES), LANES)
        f, v, n = fb[:, lanes], tb[:, lanes], nb[:, lanes]
        e, af, at = f - v, f - n, v - n

        def total_of(u):
            return jnp.sum(u, axis=0, keepdims=True)

        sums = jnp.concatenate(
            [jnp.zeros((4, LANES), jnp.float32), total_of(e * e), total_of(af * at), total_of(af * af), total_of(at * at)],
            axis=0,
        )
        sums = sums * (weight[pl.ds(lat * slots + t, 1), :] * float(total))
        pick = (field_rows == field[pl.ds(t, 1), :]).astype(jnp.float32)
        return carry + lax.dot_general(
            sums, pick, (((1,), (1,)), ((), ())),
            precision=lax.Precision.HIGHEST, preferred_element_type=jnp.float32,
        )

    skill_sums = lax.fori_loop(0, tiles, skill_tile, jnp.zeros((8, LANES), jnp.float32))
    acc[n_rows - 8 : n_rows, :] = skill_sums

    out_rows = lax.broadcasted_iota(jnp.int32, (n_rows, LANES), 0)

    def put(group, a, y):
        y = jnp.concatenate([y, pad], axis=0)
        hi = y.astype(jnp.bfloat16)
        lo = (y - hi.astype(jnp.float32)).astype(jnp.bfloat16)
        at = group * 2 * LANES + a * LANES
        stack[:depth, at : at + LANES] = hi
        stack[depth : 2 * depth, at : at + LANES] = lo
        stack[2 * depth :, at : at + LANES] = hi

    def product(r, start, width):
        return jnp.dot(tab[r], stack[:, start : start + width], preferred_element_type=jnp.float32)

    def process(c, slot):
        for a in range(2):
            x = [rx[a, c, q] for q in range(4)]
            s02, s13 = x[0] + x[2], x[1] + x[3]
            put(0, a, s02 + s13)
            put(1, a, s02 - s13)
            put(2, a, x[0] - x[2])
            put(3, a, x[1] - x[3])
        w = weight[pl.ds(lat * slots + slot, 1), :]
        for r in range(4):
            if r % 2 == 0:
                both = product(r, (r // 2) * 2 * LANES, 2 * LANES)
                re, im = both[:per_class], both[per_class:]
            else:
                both = product(r, 4 * LANES, 4 * LANES)
                u, v = both[:per_class], both[per_class:]
                g = 1.0 if r == 1 else -1.0
                re = u[:, : 2 * LANES] - g * v[:, 2 * LANES :]
                im = v[:, : 2 * LANES] + g * u[:, 2 * LANES :]
            for curve in range(3):
                if curve == 2:
                    a, b = re[:, :LANES] - re[:, LANES:], im[:, :LANES] - im[:, LANES:]
                else:
                    cut = slice(curve * LANES, (curve + 1) * LANES)
                    a, b = re[:, cut], im[:, cut]
                pbuf.at[curve][pl.ds(r, per_class, stride=4), :] = (a * a + b * b) * w
        fld = field[pl.ds(slot, 1), :]
        for curve in range(3):
            power = pbuf[curve]
            hi = power.astype(jnp.bfloat16)
            lo = (power - hi.astype(jnp.float32)).astype(jnp.bfloat16)
            pick = (out_rows == jnp.where(fld >= 0, fld + FIELDS * curve, -1)).astype(jnp.float32).astype(jnp.bfloat16)
            part = lax.dot_general(
                jnp.concatenate([pick, pick], axis=1), jnp.concatenate([hi, lo], axis=1),
                (((1,), (1,)), ((), ())), preferred_element_type=jnp.float32,
            )
            for t in range(part.shape[1] // LANES):
                acc[t * n_rows : (t + 1) * n_rows, :] += part[:, t * LANES : (t + 1) * LANES]

    def take_tile(c):
        for a in range(2):
            own[a, c].wait()
            for p in range(1, n_lon):
                sends[a, c, p].wait_recv()
        process(c, lon * own_tiles + c)

    def take_piece():
        for a in range(2):
            for p in range(1, n_lon):
                sends[a, "piece", p].wait_recv()
        gap = jnp.zeros((LANES - piece, depth), jnp.float32)
        for a in range(2):
            pr[a, lon] = ps[a, lon]
            for q in range(n_lon):
                rx[a, own_tiles, q] = jnp.concatenate([pr[a, q], gap], axis=0).T[:rows]
        process(own_tiles, tiles + lon)

    for c in loads[5:]:
        c.wait()
    take_tile(0)
    take_tile(1)
    take_piece()
    for c in range(2, own_tiles):
        take_tile(c)

    size = acc.shape[0]
    s_half, s_quart = size // 2, size // (2 * n_lon)
    s_piece = s_quart // n_z

    def exchange(index, src, dst, device):
        copy = pltpu.make_async_remote_copy(
            src_ref=src, dst_ref=dst, send_sem=ss.at[index], recv_sem=sr.at[index],
            device_id=device, device_id_type=MESH,
        )
        copy.start()
        return copy

    def part(start, length):
        return pl.ds(pl.multiple_of(start, 8), length)

    def quarter(j):
        return flips[j] * s_quart

    near_first, far_first = (1, 2, 3), (3, 1, 2)
    cross = {
        j: exchange(
            j, acc.at[part((1 - core) * s_half + quarter(j), s_quart)],
            r0.at[part(quarter(j), s_quart)], sibling,
        )
        for j in (*far_first, 0)
    }
    base = n_lon
    over_lon = {}
    for j in (*far_first, 0):
        cross[j].wait_recv()
        rows_j = part(quarter(j), s_quart)
        half[rows_j, :] = acc[part(core * s_half + quarter(j), s_quart), :] + r0[rows_j, :]
        if j > 0:
            for p in range(n_z):
                at = p * s_piece
                over_lon[j, p] = exchange(
                    base + (j - 1) * n_z + p, half.at[part(quarter(j) + at, s_piece)],
                    r1.at[j - 1, part(at, s_piece)], lon_peer(j),
                )
    base += (n_lon - 1) * n_z
    over_z = {}
    z_order = (2, 1, 3)
    for s in range(n_z):
        for j in range(1, n_lon):
            over_lon[j, s].wait_recv()
        rows_s = pl.ds(s * s_piece, s_piece)
        r2[z, rows_s, :] = (
            half[part(quarter(0) + s * s_piece, s_piece), :] + r1[0, rows_s, :] + r1[1, rows_s, :] + r1[2, rows_s, :]
        )
        for p in z_order:
            over_z[p, s] = exchange(base + (p - 1) * n_z + s, r2.at[z, rows_s], r2.at[z, rows_s], z_peer(p))
    base += (n_z - 1) * n_z
    quarter_at = core * s_half + quarter(0)
    back_lon = {}
    for s in range(n_z):
        for p in z_order:
            over_z[p, s].wait_recv()
        rows_s = pl.ds(s * s_piece, s_piece)
        mine = part(quarter_at + s * s_piece, s_piece)
        full[mine, :] = r2[0, rows_s, :] + r2[1, rows_s, :] + r2[2, rows_s, :] + r2[3, rows_s, :]
        for j in far_first:
            back_lon[j, s] = exchange(base + (j - 1) * n_z + s, full.at[mine], full.at[mine], lon_peer(j))
    base += (n_lon - 1) * n_z
    back_core = {}
    outs = []

    def put_out(index, rows_out):
        copy = pltpu.make_async_copy(full.at[rows_out], result.at[rows_out], load_sem.at[index])
        copy.start()
        outs.append(copy)

    for j in (0, *near_first):
        if j > 0:
            for p in range(n_z):
                back_lon[j, p].wait_recv()
        rows_j = part(core * s_half + quarter(j), s_quart)
        back_core[j] = exchange(base + j, full.at[rows_j], full.at[rows_j], sibling)
        put_out(j, rows_j)
    for j, c in back_core.items():
        c.wait_recv()
        put_out(n_lon + j, part((1 - core) * s_half + quarter(j), s_quart))
    for group in (cross, over_lon, over_z, back_lon, back_core):
        for c in group.values():
            c.wait_send()
    for c in sends.values():
        c.wait_send()

    for c in outs:
        c.wait()


def finish(waves, full, energy, rms, corr):
    n_rows = 3 * FIELDS + 4
    for t in range(-(-waves // LANES)):
        width = min(LANES, waves - t * LANES)
        for curve in range(3):
            at = t * n_rows + curve * FIELDS
            energy[curve, :, t * LANES : t * LANES + width] = full[at : at + FIELDS, :width]
    means = full[n_rows - 4 : n_rows, :]
    m_ee, m_ft, m_ff, m_tt = means[0:1], means[1:2], means[2:3], means[3:4]
    rms[...] = jnp.sqrt(m_ee)[0, :FIELDS]
    corr[...] = (m_ft / jnp.sqrt((m_ff + epsilon) * (m_tt + epsilon)))[0, :FIELDS]


def fused(lat_devices, lon_devices, predicted_state, verified_state, normal_state):
    rows, cols = predicted_state.shape
    total = rows * lon_devices
    waves = total // 2 + 1
    tab_hi, tab_lo, field, weight = plan_constants(rows, cols, lat_devices, lon_devices)
    depth = tab_hi.shape[2]
    per_class = tab_hi.shape[1] // 2
    tiles = cols // LANES
    own_tiles = tiles // lon_devices
    piece = LANES // lon_devices
    spread = -(-4 * per_class // LANES) * LANES
    n_rows = 3 * FIELDS + 4
    n_z = lat_devices // 2
    unit = 8 * lat_devices * lon_devices
    size = -(-(spread // LANES) * n_rows // unit) * unit
    f32, b16 = jnp.float32, jnp.bfloat16
    copies = 3 * lon_devices * n_z
    dma = pltpu.SemaphoreType.DMA
    scratch = [
        pltpu.VMEM((rows, cols), f32), pltpu.VMEM((rows, cols), f32), pltpu.VMEM((rows, cols), f32),
        pltpu.VMEM((2, own_tiles + 1, lon_devices, rows, LANES), f32),
        pltpu.VMEM((2, lon_devices, piece, depth), f32),
        pltpu.VMEM((2, lon_devices, piece, depth), f32),
        pltpu.VMEM((3 * depth, 8 * LANES), b16),
        pltpu.VMEM((3, spread, LANES), f32),
        pltpu.VMEM((size, LANES), f32),
        pltpu.VMEM((size // 2, LANES), f32), pltpu.VMEM((size // 2, LANES), f32),
        pltpu.VMEM((lon_devices - 1, size // (2 * lon_devices), LANES), f32),
        pltpu.VMEM((n_z, size // (2 * lon_devices), LANES), f32),
        pltpu.VMEM((size, LANES), f32),
        dma((8,)), dma((2, own_tiles)),
        dma((2, own_tiles, lon_devices - 1)), dma((2, own_tiles, lon_devices - 1)),
        dma((2, lon_devices - 1)), dma((2, lon_devices - 1)),
        dma((copies,)), dma((copies,)),
        pltpu.VMEM((4, 2 * per_class, 3 * depth), b16),
        pltpu.VMEM(field.shape, jnp.int32), pltpu.VMEM(weight.shape, f32),
    ]
    any_spec = pl.BlockSpec(memory_space=pl.ANY)
    vmem = pl.BlockSpec(memory_space=pltpu.VMEM)
    dims = (rows, cols, lat_devices, lon_devices, total)
    summed = pl.pallas_call(
        functools.partial(kernel, dims),
        out_shape=jax.ShapeDtypeStruct((size, LANES), f32),
        in_specs=[any_spec] * 7,
        out_specs=any_spec,
        scratch_shapes=scratch,
        compiler_params=pltpu.CompilerParams(
            collective_id=0, has_side_effects=True, vmem_limit_bytes=60_000_000
        ),
    )(predicted_state, verified_state, normal_state, jnp.asarray(tab_hi), jnp.asarray(tab_lo), jnp.asarray(field), jnp.asarray(weight))
    return pl.pallas_call(
        functools.partial(finish, waves),
        out_shape=(
            jax.ShapeDtypeStruct((3, FIELDS, waves), f32),
            jax.ShapeDtypeStruct((FIELDS,), f32),
            jax.ShapeDtypeStruct((FIELDS,), f32),
        ),
        in_specs=[vmem],
        out_specs=(vmem, vmem, vmem),
    )(summed)


def solution(mesh):
    in_specs = (P("lon", "lat"), P("lon", "lat"), P("lon", "lat"))
    out_specs = (P(), P(), P())
    n_lat, n_lon = mesh.shape["lat"], mesh.shape["lon"]

    def body(predicted_state, verified_state, normal_state):
        rows, cols = predicted_state.shape
        fits = (
            n_lon == 4 and n_lat == 8 and rows % 8 == 0
            and cols % LANES == 0 and cols // LANES % n_lon == 1 and cols // LANES // n_lon >= 2
        )
        if fits:
            return fused(n_lat, n_lon, predicted_state, verified_state, normal_state)
        return local(predicted_state, verified_state, normal_state)

    return jax.shard_map(body, mesh=mesh, in_specs=in_specs, out_specs=out_specs, check_vma=False)
```
